512 devices in a mesh: ctx: 32 (over y, z_lo), ep: 16 (over z_hi, x, core).
Axes of the slice: x: 4, y: 8, z: 8 (z_hi: 2, z_lo: 4; z = z_hi * 4 + z_lo), core: 2. Of those that a mesh axis runs over, the one named last changes fastest.
Arguments:
- queries: bfloat16 [16, 4096, 2048], P('ep', 'ctx'), may hold values from -100 to 100
- keys: bfloat16 [16, 4096, 2048], P('ep', 'ctx'), may hold values from -4 to 4
- values: bfloat16 [16, 4096, 2048], P('ep', 'ctx'), may hold values from -6 to 6
- doc_ids: int32 [16, 4096], P('ep', 'ctx'), may hold values from 0 to 31, never falling along the last dimension, each value on 1 to 256 neighbouring positions
- routes: int32 [16, 4096, 1], P('ep', 'ctx'), may hold values from 0 to 63
- route_weight: float32 [16, 4096, 1], P('ep', 'ctx'), may hold values from 0.2 to 1
- norm_gain: float32 [2048], replicated, may hold values from 0.25 to 1.75
- w_gate: bfloat16 [2048, 90112], P(None, ('ctx', 'ep')), may hold values from -0.125 to 0.125
- w_up: bfloat16 [2048, 90112], P(None, ('ctx', 'ep')), may hold values from -0.125 to 0.125
- w_down: bfloat16 [90112, 2048], P(('ctx', 'ep')), may hold values from -0.15625 to 0.15625
- grad_out: bfloat16 [16, 4096, 2048], P('ep', 'ctx'), may hold values from -6 to 6
Outputs:
- grad_in: bfloat16 [16, 4096, 2048], P('ep', 'ctx')
The draws below stay inside these ranges and needn't reach their ends.
Inputs may be any that keep to these rules, and one draw needn't show every extreme that they name: `doc_ids`: no document has more than 256 tokens; ids never fall along a sequence.
All inputs are finite; a program needn't handle non-finite values.
Results may differ from the reference program's by a relative error of at most 0.0086.
Values may be sent and summed in bfloat16 or wider, within the bound.
A program may use at most 64 MiB of HBM per device.

```python
import math
import jax
import jax.numpy as jnp
import numpy as np
from jax import lax

D = 2048
HEADS = 16
HEAD = 128
EXPERTS = 64
FF = 1408
ROUTES = 1
CAP = 2
STRETCH = 128
SEQS = 16
LENGTH = 4096
DOC_MAX = 256
DOCS = 32
REACH = 2
SLICE = 176
SLICES = 8


def pair_fields(key):
    query_key = jax.random.fold_in(key, 101)
    key_key = jax.random.fold_in(key, 202)
    field_shape = (SEQS, LENGTH, D)
    drawn_queries = jax.random.truncated_normal(query_key, -4.0, 4.0, field_shape, jnp.float32)
    drawn_keys = jax.random.truncated_normal(key_key, -4.0, 4.0, field_shape, jnp.float32)
    return (drawn_queries, drawn_keys)


def draw_queries(key, part):
    return pair_fields(key)[0].astype(jnp.bfloat16)


def draw_keys(key, part):
    return pair_fields(key)[1].astype(jnp.bfloat16)


def block_levels(rng, extent, split, smallest, high):
    level = 1.0
    for position, blocks in split:
        steps = jax.random.uniform(jax.random.fold_in(jax.random.fold_in(rng, 6), position), (blocks,), jnp.float32, smallest / len(split), high / len(split))
        level = level * jnp.repeat(jnp.exp(steps), extent[position] // blocks).reshape((-1,) + (1,) * (len(extent) - 1 - position))
    return level


def picks_of(key, rows, count, top, lift):
    order = jax.random.permutation(jax.random.fold_in(key, 1), count)
    boost = order
    for power in range(3):
        boost = boost * boost // count
    boost = boost * lift // count
    tickets = jax.random.randint(jax.random.fold_in(key, 2), (rows, count), 0, 4096) + boost
    holders = jax.random.permutation(jax.random.fold_in(key, 3), rows)[jnp.arange(count) % rows]
    tickets = jnp.where(jnp.arange(rows)[:, None] == holders[None, :], 1 << 14, tickets)
    priority = tickets * count + jnp.arange(count)
    return lax.top_k(priority.astype(jnp.int32), top)[1].astype(jnp.int32)


def split_up(amount, total, most, lean):
    portions = [(1 << 20) // math.isqrt(standing ** lean) + 1 for standing in range(2, amount + 1)]
    surplus, given = total - most - (amount - 1), [1] * (amount - 1)
    while surplus > 0:
        movable = [i for i in range(amount - 1) if given[i] < most]
        mass, budget = sum([portions[i] for i in movable]), surplus
        for i in movable:
            extra = min(most - given[i], max(1, budget * portions[i] // mass), surplus)
            given[i] = given[i] + extra
            surplus = surplus - extra
    return np.array([most] + given)


def uneven_parts(stream_key, count, total, bound, skew):
    if count == 2:
        one = jax.random.randint(stream_key, (), max(1, total - bound), min(bound, total - 1) + 1)
        return jnp.stack([one, total - one])
    lengths = jnp.asarray(split_up(count, total, bound, skew), jnp.int32)
    couples = (count - 1) // 2
    giver, receiver = lengths[1:1 + 2 * couples:2], lengths[2:2 + 2 * couples:2]
    margin = jnp.minimum(giver - 1, bound - receiver)
    moved = jax.random.randint(jax.random.fold_in(stream_key, 1), (couples,), 0, 1 << 20) % (margin + 1)
    lengths = lengths.at[1:1 + 2 * couples:2].set(giver - moved).at[2:2 + 2 * couples:2].set(receiver + moved)
    return lengths[jax.random.permutation(jax.random.fold_in(stream_key, 2), count)]


def centred(stream_key, shape, scale, most, cuts=(), held_as=jnp.bfloat16):
    values = scale * jax.random.normal(stream_key, shape, jnp.float32)
    if cuts:
        values = values * block_levels(stream_key, shape, cuts, -0.22, 0.18)
    return jnp.clip(values, -most, most).astype(held_as)


def setup_inputs(seed: int = 0) -> dict:
    key_of = jax.random.split(jax.random.key(seed), 12)
    queries = draw_queries(jax.random.fold_in(key_of[11], 71), 0)
    keys = draw_keys(jax.random.fold_in(key_of[11], 71), 0)
    values = centred(key_of[2], (SEQS, LENGTH, D), 1.0, 6.0, ((0, 16), (1, 32)))
    doc_ids = jax.vmap(lambda own: jnp.searchsorted(jnp.cumsum(uneven_parts(own, DOCS, LENGTH, DOC_MAX, 2)), jnp.arange(LENGTH), side="right"))(jax.random.split(key_of[3], SEQS)).reshape((SEQS, LENGTH)).astype(jnp.int32)
    routes = picks_of(key_of[4], SEQS * LENGTH, EXPERTS, ROUTES, 256).reshape((SEQS, LENGTH, ROUTES))
    route_weight = jnp.clip(0.2 + 0.8 * jax.random.uniform(key_of[5], (SEQS, LENGTH, ROUTES), jnp.float32) ** block_levels(key_of[5], (SEQS, LENGTH, ROUTES), ((0, 16), (1, 32)), -0.2, 0.2), 0.2, 1.0)
    norm_gain = jnp.clip(1.0 + 0.15 * jax.random.normal(key_of[6], (D,), jnp.float32), 0.25, 1.75)
    w_gate = centred(key_of[7], (D, EXPERTS * FF), D ** -0.5, 0.125, ((1, 512),))
    w_up = centred(key_of[8], (D, EXPERTS * FF), D ** -0.5, 0.125, ((1, 512),))
    w_down = centred(key_of[9], (EXPERTS * FF, D), FF ** -0.5, 0.15625, ((0, 512),))
    grad_out = centred(key_of[10], (SEQS, LENGTH, D), 1.0, 6.0, ((0, 16), (1, 32)))
    return {"queries": queries, "keys": keys, "values": values, "doc_ids": doc_ids, "routes": routes, "route_weight": route_weight, "norm_gain": norm_gain, "w_gate": w_gate, "w_up": w_up, "w_down": w_down, "grad_out": grad_out}


def attend_sequence(operands):
    seq_queries, seq_keys, seq_values, seq_tags = operands
    padding = REACH * STRETCH
    keys_padded = jnp.concatenate([jnp.zeros((padding, D), seq_keys.dtype), seq_keys])
    values_padded = jnp.concatenate([jnp.zeros((padding, D), seq_values.dtype), seq_values])
    tags_padded = jnp.concatenate([jnp.full((padding,), -1, jnp.int32), seq_tags])
    score_scale = 1.0 / math.sqrt(HEAD)

    def one_block(block_index):
        first_row = block_index * STRETCH
        query_block = lax.dynamic_slice_in_dim(seq_queries, first_row, STRETCH, 0).astype(jnp.float32).reshape(STRETCH, HEADS, HEAD)
        key_block = lax.dynamic_slice_in_dim(keys_padded, first_row, padding + STRETCH, 0).astype(jnp.float32).reshape(padding + STRETCH, HEADS, HEAD)
        value_block = lax.dynamic_slice_in_dim(values_padded, first_row, padding + STRETCH, 0).astype(jnp.float32).reshape(padding + STRETCH, HEADS, HEAD)
        query_tags = lax.dynamic_slice_in_dim(seq_tags, first_row, STRETCH, 0)
        key_tags = lax.dynamic_slice_in_dim(tags_padded, first_row, padding + STRETCH, 0)
        scores = jnp.einsum('qhd,khd->hqk', query_block, key_block) * score_scale
        query_pos = jnp.arange(STRETCH, dtype=jnp.int32)[:, None] + padding
        key_pos = jnp.arange(padding + STRETCH, dtype=jnp.int32)[None, :]
        visible = (query_tags[:, None] == key_tags[None, :]) & (key_pos <= query_pos)
        scores = jnp.where(visible[None], scores, -1e+30)
        row_max = lax.optimization_barrier(jnp.max(scores, axis=-1, keepdims=True))
        weights_exp = jnp.exp(scores - row_max)
        probs = (weights_exp / lax.optimization_barrier(jnp.sum(weights_exp, axis=-1, keepdims=True))).astype(jnp.bfloat16)
        attended = jnp.einsum('hqk,khd->qhd', probs.astype(jnp.float32), value_block)
        return attended.reshape(STRETCH, D).astype(jnp.bfloat16)
    blocks = lax.map(one_block, jnp.arange(LENGTH // STRETCH, dtype=jnp.int32))
    return blocks.reshape(LENGTH, D)

def reference(queries, keys, values, doc_ids, routes, route_weight, norm_gain, w_gate, w_up, w_down, grad_out):
    hidden_bf = lax.map(attend_sequence, (queries, keys, values, doc_ids + 1))
    hidden = lax.optimization_barrier(hidden_bf).astype(jnp.float32)
    inv_rms = lax.rsqrt(lax.optimization_barrier(jnp.mean(hidden * hidden, axis=-1, keepdims=True)) + 1e-06)
    normed = (hidden * inv_rms * norm_gain).astype(jnp.bfloat16)
    grad_f = grad_out.astype(jnp.float32)
    grad_rows = (route_weight[..., 0:1] * grad_f).astype(jnp.bfloat16)
    block_count = SEQS * LENGTH // STRETCH
    expert_ids = routes[..., 0].reshape(block_count, STRETCH)
    onehot = (expert_ids[..., None] == jnp.arange(EXPERTS, dtype=jnp.int32)).astype(jnp.int32)
    running = jnp.cumsum(onehot, axis=1)
    slot_rank = lax.optimization_barrier(jnp.sum(onehot * (running - 1), axis=-1)).astype(jnp.int32)
    kept_rows = slot_rank < CAP
    slot_index = jnp.where(kept_rows, slot_rank, CAP).astype(jnp.int32)
    block_ids = jnp.broadcast_to(jnp.arange(block_count, dtype=jnp.int32)[:, None], (block_count, STRETCH))
    slot_inputs = jnp.zeros((EXPERTS, block_count, CAP + 1, D), jnp.bfloat16)
    slot_inputs = slot_inputs.at[expert_ids, block_ids, slot_index].set(normed.reshape(block_count, STRETCH, D))[:, :, :CAP]
    slot_grads = jnp.zeros((EXPERTS, block_count, CAP + 1, D), jnp.bfloat16)
    slot_grads = slot_grads.at[expert_ids, block_ids, slot_index].set(grad_rows.reshape(block_count, STRETCH, D))[:, :, :CAP]
    gate_table = w_gate.reshape(D, EXPERTS, FF).transpose(1, 0, 2)
    up_table = w_up.reshape(D, EXPERTS, FF).transpose(1, 0, 2)
    down_table = w_down.reshape(EXPERTS, FF, D)

    def expert_term(operands):
        rows_in, rows_grad, gate_w, up_w, down_w = operands
        row_count = block_count * CAP
        rows_in = rows_in.reshape(row_count, D)
        rows_grad = rows_grad.reshape(row_count, D)
        gate_pre = jnp.dot(rows_in, gate_w, preferred_element_type=jnp.float32)
        up_pre = jnp.dot(rows_in, up_w, preferred_element_type=jnp.float32)
        grad_act = jnp.dot(rows_grad, down_w.T, preferred_element_type=jnp.float32)
        sigmoid_gate = jax.nn.sigmoid(gate_pre)
        gate_act = gate_pre * sigmoid_gate
        act_slope = sigmoid_gate * (1.0 + gate_pre * (1.0 - sigmoid_gate))
        grad_gate = (grad_act * up_pre * act_slope).astype(jnp.bfloat16)
        grad_up = (grad_act * gate_act).astype(jnp.bfloat16)
        partial_gate = jnp.einsum('rkw,dkw->rkd', grad_gate.astype(jnp.float32).reshape(row_count, SLICES, SLICE), gate_w.astype(jnp.float32).reshape(D, SLICES, SLICE))
        partial_up = jnp.einsum('rkw,dkw->rkd', grad_up.astype(jnp.float32).reshape(row_count, SLICES, SLICE), up_w.astype(jnp.float32).reshape(D, SLICES, SLICE))
        partial_bf = lax.optimization_barrier((partial_gate + partial_up).astype(jnp.bfloat16))
        summed = lax.optimization_barrier(jnp.sum(partial_bf.astype(jnp.float32), axis=1)).astype(jnp.bfloat16)
        return summed.reshape(block_count, CAP, D)
    expert_grad = lax.map(expert_term, (slot_inputs, slot_grads, gate_table, up_table, down_table))
    expert_grad = lax.optimization_barrier(expert_grad)
    gathered = expert_grad[expert_ids, block_ids, jnp.clip(slot_rank, 0, CAP - 1).astype(jnp.int32)]
    grad_normed = gathered.astype(jnp.float32) * kept_rows[..., None].astype(jnp.float32)
    grad_normed = grad_normed.reshape(SEQS, LENGTH, D)
    gained = grad_normed * norm_gain
    grad_in = grad_f + inv_rms * gained - hidden * inv_rms * inv_rms * inv_rms * lax.optimization_barrier(jnp.mean(hidden * gained, axis=-1, keepdims=True))
    return grad_in.astype(jnp.bfloat16)
```

```python
import functools
import math

import jax
import jax.numpy as jnp
from jax import lax
from jax.experimental import pallas as pl
from jax.experimental.pallas import tpu as pltpu
from jax.sharding import PartitionSpec as P

HEADS = 16
HEAD = 128
CAP = 2
ZL = 4
ZH = 2
XS = 4
CORES = 2
SLICES = XS * CORES
GROUP_HEADS = 2
LEAD = 3
HALVES = 2

F32 = jnp.float32
BF16 = jnp.bfloat16
MESH = pl.DeviceIdType.MESH


def nn(a, b):
    return lax.dot_general(a, b, (((1,), (0,)), ((), ())), preferred_element_type=F32)


def nt(a, b):
    return lax.dot_general(a, b, (((1,), (1,)), ((), ())), preferred_element_type=F32)


def scratch_of(tokens, width, slice_cols, ys):
    zs = ZL * ZH
    slots = ys * zs * CAP
    cols = GROUP_HEADS * HEAD
    groups = width // cols
    hidden_units = SLICES * slice_cols
    half = hidden_units // HALVES
    dma = pltpu.SemaphoreType.DMA
    chunked = pltpu.VMEM((groups, slots, cols), BF16)
    flat = pltpu.VMEM((slots, width), BF16)
    weights = pltpu.VMEM((hidden_units, width), BF16)
    return dict(
        q=pltpu.VMEM((groups, tokens, cols), BF16),
        kv=pltpu.VMEM((3, 2, groups, tokens, cols), BF16),
        tags=pltpu.VMEM((2, 1, tokens), jnp.int32),
        go=pltpu.VMEM((tokens, width), BF16),
        bias=pltpu.VMEM((3, tokens, tokens), F32),
        pick=pltpu.VMEM((slots, tokens), BF16),
        place=pltpu.VMEM((tokens, slots), BF16),
        perm_f=pltpu.VMEM((slots, slots), BF16),
        perm_r=pltpu.VMEM((slots, slots), BF16),
        g_send=flat, g_z=flat, g_mid=flat, g_y=flat,
        hid=pltpu.VMEM((groups, tokens, cols), BF16),
        h_send=chunked, h_z=chunked, h_mid=chunked, h_y=chunked,
        wg=weights, wu=weights, wd=weights,
        normed=flat,
        d_gate=pltpu.VMEM((HALVES, slots, half), BF16),
        d_up=pltpu.VMEM((HALVES, slots, half), BF16),
        r_send=chunked, r_y=chunked, r_mid=chunked, r_z=chunked,
        gained=pltpu.VMEM((groups, tokens, cols), F32),
        out_v=pltpu.VMEM((groups, tokens, cols), BF16),
        load_q=dma, load_kv=dma, load_go=dma, load_w=dma((3,)), store=dma,
        kv_s=dma((2, 2, groups)), kv_r=dma((2, 2, groups)),
        tag_s=dma((2,)), tag_r=dma((2,)),
        gz_s=dma, gz_r=dma, gy_s=dma, gy_r=dma,
        hz_s=dma((groups,)), hz_r=dma((groups,)), hy_s=dma((groups,)), hy_r=dma((groups,)),
        ry_s=dma((groups,)), ry_r=dma((groups,)), rz_s=dma((groups,)), rz_r=dma((groups,)),
        w_s=dma((3, 8)), w_r=dma((3, 8)),
    )


def kernel(
    names, doc_ref, route_ref, rw_ref, gain_ref,
    q_hbm, k_hbm, v_hbm, go_hbm, wg_hbm, wu_hbm, wd_hbm, out_hbm, *scratch,
):
    s = dict(zip(names, scratch))
    groups, tokens, cols = s["q"].shape
    slots = s["pick"].shape[0]
    width = groups * cols
    slice_cols = wd_hbm.shape[0]
    half = s["d_gate"].shape[2]
    ctx, ep = lax.axis_index("ctx"), lax.axis_index("ep")
    ctxs = lax.axis_size("ctx")
    ys, zs = ctxs // ZL, ZL * ZH
    y, z_lo = ctx // ZL, ctx % ZL
    z_hi, x, core = ep // (XS * CORES), (ep // CORES) % XS, ep % CORES
    z = z_hi * ZL + z_lo
    z_rows, y_rows = ys * CAP, zs * CAP

    def z_peer(t):
        return {"ctx": y * ZL + t % ZL, "ep": (t // ZL) * (XS * CORES) + x * CORES + core}

    def y_peer(t):
        return {"ctx": t * ZL + z_lo, "ep": ep}

    def x_peer(t, c):
        return {"ctx": ctx, "ep": z_hi * (XS * CORES) + (t % XS) * CORES + c}

    after = {"ctx": (ctx + 1) % ctxs, "ep": ep}
    before = {"ctx": (ctx + ctxs - 1) % ctxs, "ep": ep}
    right, left = x_peer(x + 1, core), x_peer(x + XS - 1, core)
    twin = x_peer(x, 1 - core)

    def order(count):
        steps = []
        for i in range(1, count // 2 + 1):
            steps.append(i)
            if count - i != i:
                steps.append(count - i)
        return steps

    barrier = pltpu.get_barrier_semaphore()
    peers = [after, before, right, left, twin]
    peers += [z_peer((z + i) % zs) for i in order(zs)]
    peers += [y_peer((y + i) % ys) for i in order(ys)]
    for peer in peers:
        pl.semaphore_signal(barrier, inc=1, device_id=peer, device_id_type=MESH)

    def local(src, dst, sem):
        pltpu.make_async_copy(src, dst, sem).start()

    def wait(ref, sem):
        pltpu.make_async_copy(ref, ref, sem).wait()

    def send(src, dst, s_sem, r_sem, peer):
        pltpu.make_async_remote_copy(
            src_ref=src, dst_ref=dst, send_sem=s_sem, recv_sem=r_sem,
            device_id=peer, device_id_type=MESH,
        ).start()

    def exchange(src, dst, rows, count, mine, peer, s_sem, r_sem):
        own = pl.ds(pl.multiple_of(mine * rows, rows), rows)
        for i in order(count):
            t = (mine + i) % count
            there = pl.ds(pl.multiple_of(t * rows, rows), rows)
            send(src.at[there], dst.at[own], s_sem, r_sem, peer(t))
        local(src.at[own], dst.at[own], r_sem)

    def sent(src, rows, count, s_sem):
        wait(src.at[pl.ds(0, rows * (count - 1))], s_sem)

    def col(g):
        return pl.ds(pl.multiple_of(g * cols, cols), cols)

    local(go_hbm.at[0], s["go"], s["load_go"])
    own_rows = pl.ds(0, slice_cols)
    for a, (ref, name) in enumerate(((wg_hbm, "wg"), (wu_hbm, "wu"), (wd_hbm, "wd"))):
        local(ref, s[name].at[own_rows], s["load_w"].at[a])

    @pl.loop(0, groups)
    def _(g):
        local(q_hbm.at[0, :, col(g)], s["q"].at[g], s["load_q"])
        local(k_hbm.at[0, :, col(g)], s["kv"].at[0, 0, g], s["load_kv"])
        local(v_hbm.at[0, :, col(g)], s["kv"].at[0, 1, g], s["load_kv"])

    def grid(shape, axis):
        return lax.broadcasted_iota(jnp.int32, shape, axis)

    def across(row):
        return jnp.transpose(jnp.broadcast_to(row.astype(F32), (tokens, tokens)))

    def onehot(mask):
        return jnp.where(mask, 1.0, 0.0).astype(BF16)

    square = (tokens, tokens)
    route_row = route_ref[...].astype(F32)
    same = (jnp.broadcast_to(route_row, square) == across(route_row)) & (
        grid(square, 0) < grid(square, 1)
    )
    rank = jnp.sum(jnp.where(same, 1.0, 0.0), axis=0, keepdims=True).astype(jnp.int32)
    expert = route_ref[...]
    bits_zh, bits_zl = ZH.bit_length() - 1, ZL.bit_length() - 1
    dest_y = lax.shift_right_logical(expert, bits_zh + bits_zl)
    dest_z = (expert & (ZH - 1)) * ZL + (lax.shift_right_logical(expert, bits_zh) & (ZL - 1))
    target = jnp.where(rank < CAP, dest_z * z_rows + dest_y * CAP + rank, -1)
    s["pick"][...] = onehot(jnp.broadcast_to(target, (slots, tokens)) == grid((slots, tokens), 0))
    s["place"][...] = onehot(across(target) == grid((tokens, slots), 1).astype(F32))

    def regroup(index, outer, inner):
        bits_o, bits_i = outer.bit_length() - 1, inner.bit_length() - 1
        o = lax.shift_right_logical(index, bits_i + 1)
        i = lax.shift_right_logical(index, 1) & (inner - 1)
        return i * (outer * CAP) + o * CAP + (index & (CAP - 1))

    pairs = (slots, slots)
    s["perm_f"][...] = onehot(regroup(grid(pairs, 0), ys, zs) == grid(pairs, 1))
    s["perm_r"][...] = onehot(regroup(grid(pairs, 0), zs, ys) == grid(pairs, 1))

    pl.semaphore_wait(barrier, len(peers))

    def send_own(g):
        for part, ref in ((0, k_hbm), (1, v_hbm)):
            send(
                ref.at[0, :, col(g)], s["kv"].at[1, part, g],
                s["kv_s"].at[0, part, g], s["kv_r"].at[0, part, g], after,
            )

    for g in range(min(LEAD, groups)):
        send_own(g)
    send(doc_ref, s["tags"].at[0], s["tag_s"].at[0], s["tag_r"].at[0], after)

    gathered = (s["wg"], s["wu"], s["wd"])

    def part_of(slot):
        return pl.ds(slot * slice_cols, slice_cols)

    def weights_out(a, src):
        ref = gathered[a]
        send(src, ref.at[part_of(2)], s["w_s"].at[a, 0], s["w_r"].at[a, 0], right)
        send(src, ref.at[part_of(4)], s["w_s"].at[a, 1], s["w_r"].at[a, 1], left)
        send(src, ref.at[part_of(1)], s["w_s"].at[a, 2], s["w_r"].at[a, 2], twin)

    first_cols, last_cols = pl.ds(0, width // 2), pl.ds(width // 2, width // 2)

    def weights_relay(a):
        ref = gathered[a]
        wait(ref.at[part_of(2)], s["w_r"].at[a, 0])
        send(
            ref.at[part_of(2), first_cols], ref.at[part_of(6), first_cols],
            s["w_s"].at[a, 3], s["w_r"].at[a, 3], right,
        )
        send(ref.at[part_of(2)], ref.at[part_of(3)], s["w_s"].at[a, 5], s["w_r"].at[a, 5], twin)
        wait(ref.at[part_of(4)], s["w_r"].at[a, 1])
        send(
            ref.at[part_of(4), last_cols], ref.at[part_of(6), last_cols],
            s["w_s"].at[a, 4], s["w_r"].at[a, 4], left,
        )
        send(ref.at[part_of(4)], ref.at[part_of(5)], s["w_s"].at[a, 6], s["w_r"].at[a, 6], twin)

    def weights_last(a):
        ref = gathered[a]
        wait(ref.at[part_of(6), first_cols], s["w_r"].at[a, 3])
        wait(ref.at[part_of(6), last_cols], s["w_r"].at[a, 4])
        send(ref.at[part_of(6)], ref.at[part_of(7)], s["w_s"].at[a, 7], s["w_r"].at[a, 7], twin)

    def weights_in(a):
        ref = gathered[a]
        for slot, r in ((1, 2), (3, 5), (5, 6), (7, 7)):
            wait(ref.at[part_of(slot)], s["w_r"].at[a, r])
        for k in (0, 1, 2, 5, 6, 7):
            wait(ref.at[part_of(0)], s["w_s"].at[a, k])
        wait(ref.at[part_of(0), first_cols], s["w_s"].at[a, 3])
        wait(ref.at[part_of(0), last_cols], s["w_s"].at[a, 4])

    for a, ref in ((2, wd_hbm), (0, wg_hbm), (1, wu_hbm)):
        weights_out(a, ref)

    wait(s["go"], s["load_go"])
    weight_col = across(rw_ref[...])[:, :1]
    for g in range(groups):
        at = pl.ds(g * cols, cols)
        rows = (weight_col * s["go"][:, at].astype(F32)).astype(BF16)
        s["g_send"][:, at] = nn(s["pick"][...], rows).astype(BF16)
    exchange(s["g_send"], s["g_z"], z_rows, zs, z, z_peer, s["gz_s"], s["gz_r"])

    wait(s["q"], s["load_q"])
    wait(s["kv"].at[0], s["load_kv"])
    scale = 1.0 / math.sqrt(HEAD)

    def attend(g):
        for h in range(GROUP_HEADS):
            at = slice(h * HEAD, (h + 1) * HEAD)
            query = s["q"][g][:, at]
            scores = [
                nt(query, s["kv"][d, 0, g][:, at]) * scale + s["bias"][d] for d in range(3)
            ]
            top = jnp.max(
                jnp.maximum(jnp.maximum(scores[0], scores[1]), scores[2]), axis=-1, keepdims=True
            )
            raised = [jnp.exp(one - top) for one in scores]
            total = jnp.sum(raised[0] + raised[1] + raised[2], axis=-1, keepdims=True)
            share = 1.0 / total
            mixed = None
            for d in range(3):
                term = nn((raised[d] * share).astype(BF16), s["kv"][d, 1, g][:, at])
                mixed = term if mixed is None else mixed + term
            s["hid"][g, :, at] = mixed.astype(BF16)
        s["h_send"][g] = nn(s["pick"][...], s["hid"][g]).astype(BF16)

    @pl.loop(0, groups + 3)
    def _(step):
        @pl.when(step < groups)
        def _():
            for part in range(2):
                here = s["kv"].at[1, part, step]
                wait(here, s["kv_r"].at[0, part, step])
                send(
                    here, s["kv"].at[2, part, step],
                    s["kv_s"].at[1, part, step], s["kv_r"].at[1, part, step], after,
                )

        @pl.when(step + LEAD < groups)
        def _():
            send_own(step + LEAD)

        @pl.when(step == 0)
        def _():
            wait(s["tags"].at[0], s["tag_r"].at[0])
            send(s["tags"].at[0], s["tags"].at[1], s["tag_s"].at[1], s["tag_r"].at[1], after)

        @pl.when(step == 1)
        def _():
            wait(s["tags"].at[1], s["tag_r"].at[1])
            doc_col = across(doc_ref[...])
            for d in range(3):
                row = doc_ref[...] if d == 0 else s["tags"][d - 1]
                seen = row.astype(F32) - jnp.where(ctx >= d, 0.0, 1e6)
                open_ = doc_col == jnp.broadcast_to(seen, square)
                if d == 0:
                    open_ = open_ & (grid(square, 1) <= grid(square, 0))
                s["bias"][d] = jnp.where(open_, 0.0, -1e30)

        @pl.when((step >= 1) & (step <= groups))
        def _():
            g = step - 1
            for part in range(2):
                wait(s["kv"].at[2, part, g], s["kv_r"].at[1, part, g])
            attend(g)
            exchange(
                s["h_send"].at[g], s["h_z"].at[g], z_rows, zs, z, z_peer,
                s["hz_s"].at[g], s["hz_r"].at[g],
            )

        @pl.when(step >= 3)
        def _():
            g = step - 3
            wait(s["h_z"].at[g], s["hz_r"].at[g])
            s["h_mid"][g] = nn(s["perm_f"][...], s["h_z"][g]).astype(BF16)
            exchange(
                s["h_mid"].at[g], s["h_y"].at[g], y_rows, ys, y, y_peer,
                s["hy_s"].at[g], s["hy_r"].at[g],
            )

        @pl.when(step == 3)
        def _():
            wait(s["g_z"], s["gz_r"])
            for g in range(groups):
                at = pl.ds(g * cols, cols)
                s["g_mid"][:, at] = nn(s["perm_f"][...], s["g_z"][:, at]).astype(BF16)
            exchange(s["g_mid"], s["g_y"], y_rows, ys, y, y_peer, s["gy_s"], s["gy_r"])

        for a, when in ((2, 2), (0, 5), (1, 8)):

            @pl.when(step == min(when, groups + 2))
            def _():
                weights_relay(a)

    squares = None
    for g in range(groups):
        one = s["hid"][g].astype(F32)
        one = jnp.sum(one * one, axis=-1, keepdims=True)
        squares = one if squares is None else squares + one
    inv_rms = lax.rsqrt(squares * (1.0 / width) + 1e-06)

    for a in (2, 0, 1):
        weights_last(a)

    squares = None
    for g in range(groups):
        wait(s["h_y"].at[g], s["hy_r"].at[g])
        one = s["h_y"][g].astype(F32)
        one = jnp.sum(one * one, axis=-1, keepdims=True)
        squares = one if squares is None else squares + one
    inv_there = lax.rsqrt(squares * (1.0 / width) + 1e-06)
    for g in range(groups):
        at = pl.ds(g * cols, cols)
        s["normed"][:, at] = (s["h_y"][g].astype(F32) * inv_there * gain_ref[:, at]).astype(BF16)
    wait(s["g_y"], s["gy_r"])
    for a in (2, 0, 1):
        wait(gathered[a].at[own_rows], s["load_w"].at[a])
        weights_in(a)

    @pl.loop(0, HALVES)
    def _(part):
        rows = pl.ds(pl.multiple_of(part * half, half), half)
        gate_pre = nt(s["normed"][...], s["wg"][rows, :])
        up_pre = nt(s["normed"][...], s["wu"][rows, :])
        grad_act = nt(s["g_y"][...], s["wd"][rows, :])
        sg = 1.0 / (1.0 + jnp.exp(-gate_pre))
        s["d_gate"][part] = (
            grad_act * up_pre * (sg * (1.0 + gate_pre * (1.0 - sg)))
        ).astype(BF16)
        s["d_up"][part] = (grad_act * (gate_pre * sg)).astype(BF16)

    @pl.loop(0, groups + 2)
    def _(step):
        @pl.when(step < groups)
        def _():
            total = None
            for part in range(HALVES):
                rows = pl.ds(part * half, half)
                for rows_in, ref in ((s["d_gate"], s["wg"]), (s["d_up"], s["wu"])):
                    term = nn(rows_in[part], ref[rows, col(step)])
                    total = term if total is None else total + term
            s["r_send"][step] = total.astype(BF16)
            exchange(
                s["r_send"].at[step], s["r_y"].at[step], y_rows, ys, y, y_peer,
                s["ry_s"].at[step], s["ry_r"].at[step],
            )

        @pl.when(step >= 2)
        def _():
            g = step - 2
            wait(s["r_y"].at[g], s["ry_r"].at[g])
            s["r_mid"][g] = nn(s["perm_r"][...], s["r_y"][g]).astype(BF16)
            exchange(
                s["r_mid"].at[g], s["r_z"].at[g], z_rows, zs, z, z_peer,
                s["rz_s"].at[g], s["rz_r"].at[g],
            )

    along = None
    for g in range(groups):
        wait(s["r_z"].at[g], s["rz_r"].at[g])
        gained = nn(s["place"][...], s["r_z"][g]) * gain_ref[:, pl.ds(g * cols, cols)]
        s["gained"][g] = gained
        one = jnp.sum(s["hid"][g].astype(F32) * gained, axis=-1, keepdims=True)
        along = one if along is None else along + one
    slope = inv_rms * inv_rms * inv_rms * (along * (1.0 / width))
    for g in range(groups):
        at = pl.ds(g * cols, cols)
        s["out_v"][g] = (
            s["go"][:, at].astype(F32)
            + inv_rms * s["gained"][g]
            - s["hid"][g].astype(F32) * slope
        ).astype(BF16)
        local(s["out_v"].at[g], out_hbm.at[0, :, at], s["store"])

    @pl.loop(0, groups)
    def _(g):
        for hop in range(2):
            for part in range(2):
                wait(s["kv"].at[hop, part, g], s["kv_s"].at[hop, part, g])
        sent(s["h_send"].at[g], z_rows, zs, s["hz_s"].at[g])
        sent(s["h_mid"].at[g], y_rows, ys, s["hy_s"].at[g])
        sent(s["r_send"].at[g], y_rows, ys, s["ry_s"].at[g])
        sent(s["r_mid"].at[g], z_rows, zs, s["rz_s"].at[g])

    for hop in range(2):
        wait(s["tags"].at[hop], s["tag_s"].at[hop])
    sent(s["g_send"], z_rows, zs, s["gz_s"])
    sent(s["g_mid"], y_rows, ys, s["gy_s"])
    wait(s["out_v"], s["store"])


def shards(
    queries, keys, values, doc_ids, routes, route_weight, norm_gain, w_gate, w_up, w_down, grad_out
):
    tokens, width = queries.shape[1:]
    ys = lax.axis_size("ctx") // ZL
    scratch = scratch_of(tokens, width, w_gate.shape[1], ys)
    small = pl.BlockSpec(memory_space=pltpu.VMEM)
    large = pl.BlockSpec(memory_space=pl.ANY)
    return pl.pallas_call(
        functools.partial(kernel, tuple(scratch)),
        out_shape=jax.ShapeDtypeStruct(grad_out.shape, BF16),
        in_specs=[small] * 4 + [large] * 7,
        out_specs=large,
        scratch_shapes=list(scratch.values()),
        compiler_params=pltpu.CompilerParams(
            collective_id=0, has_side_effects=True, vmem_limit_bytes=60 * 1024 * 1024
        ),
        name="layer",
    )(
        doc_ids,
        routes.reshape(1, tokens),
        route_weight.reshape(1, tokens),
        norm_gain.reshape(1, width),
        queries, keys, values, grad_out, w_gate.T, w_up.T, w_down,
    )


def solution(mesh):
    rows = P("ep", "ctx", None)
    in_specs = (
        rows, rows, rows, P("ep", "ctx"), rows, rows, P(),
        P(None, ("ctx", "ep")), P(None, ("ctx", "ep")), P(("ctx", "ep"), None), rows,
    )
    return jax.shard_map(shards, mesh=mesh, in_specs=in_specs, out_specs=rows, check_vma=False)
```

```python
import functools
import math

import jax
import jax.numpy as jnp
from jax import lax
from jax.experimental import pallas as pl
from jax.experimental.pallas import tpu as pltpu
from jax.sharding import PartitionSpec as P

HEADS = 16
HEAD = 128
CAP = 2
ZL = 4
ZH = 2
XS = 4
CORES = 2
SLICES = XS * CORES
GROUP_HEADS = 2
LEAD = 3
HALVES = 2

F32 = jnp.float32
BF16 = jnp.bfloat16
MESH = pl.DeviceIdType.MESH


def nn(a, b):
    return lax.dot_general(a, b, (((1,), (0,)), ((), ())), preferred_element_type=F32)


def nt(a, b):
    return lax.dot_general(a, b, (((1,), (1,)), ((), ())), preferred_element_type=F32)


def scratch_of(tokens, width, slice_cols, ys):
    zs = ZL * ZH
    slots = ys * zs * CAP
    cols = GROUP_HEADS * HEAD
    groups = width // cols
    hidden_units = SLICES * slice_cols
    half = hidden_units // HALVES
    dma = pltpu.SemaphoreType.DMA
    chunked = pltpu.VMEM((groups, slots, cols), BF16)
    flat = pltpu.VMEM((slots, width), BF16)
    weights = pltpu.VMEM((hidden_units, width), BF16)
    return dict(
        q=pltpu.VMEM((groups, tokens, cols), BF16),
        kv=pltpu.VMEM((3, 2, groups, tokens, cols), BF16),
        tags=pltpu.VMEM((2, 1, tokens), jnp.int32),
        go=pltpu.VMEM((tokens, width), BF16),
        bias=pltpu.VMEM((3, tokens, tokens), F32),
        pick=pltpu.VMEM((slots, tokens), BF16),
        place=pltpu.VMEM((2, tokens, slots), BF16),
        perm_f=pltpu.VMEM((slots, slots), BF16),
        perm_r=pltpu.VMEM((slots, slots), BF16),
        g_send=chunked, g_z=chunked, g_mid=chunked, g_y=flat,
        hid=pltpu.VMEM((groups, tokens, cols), BF16),
        h_send=chunked, h_z=chunked, h_mid=chunked, h_y=chunked,
        wg=weights, wu=weights, wd=weights,
        normed=flat,
        d_act=pltpu.VMEM((HALVES, slots, half), F32),
        d_gate=pltpu.VMEM((HALVES, slots, half), BF16),
        d_up=pltpu.VMEM((HALVES, slots, half), BF16),
        r_send=chunked, r_one=chunked, r_mid=chunked, r_two=chunked,
        gained=pltpu.VMEM((groups, tokens, cols), F32),
        out_v=pltpu.VMEM((groups, tokens, cols), BF16),
        load_q=dma, load_kv=dma, load_go=dma, load_w=dma((3,)), store=dma,
        kv_s=dma((2, 2, groups)), kv_r=dma((2, 2, groups)),
        tag_s=dma((2,)), tag_r=dma((2,)),
        gz_s=dma((groups,)), gz_r=dma((groups,)), gy_s=dma((groups,)), gy_r=dma((groups,)),
        hz_s=dma((groups,)), hz_r=dma((groups,)), hy_s=dma((groups,)), hy_r=dma((groups,)),
        r1_s=dma((groups,)), r1_r=dma((groups,)), r2_s=dma((groups,)), r2_r=dma((groups,)),
        w_s=dma((3, 8)), w_r=dma((3, 8)),
    )


def kernel(
    names, doc_ref, route_ref, rw_ref, gain_ref,
    q_hbm, k_hbm, v_hbm, go_hbm, wg_hbm, wu_hbm, wd_hbm, out_hbm, *scratch,
):
    s = dict(zip(names, scratch))
    groups, tokens, cols = s["q"].shape
    slots = s["pick"].shape[0]
    width = groups * cols
    slice_cols = wd_hbm.shape[0]
    half = s["d_gate"].shape[2]
    ctx, ep = lax.axis_index("ctx"), lax.axis_index("ep")
    ctxs = lax.axis_size("ctx")
    ys, zs = ctxs // ZL, ZL * ZH
    y, z_lo = ctx // ZL, ctx % ZL
    z_hi, x, core = ep // (XS * CORES), (ep // CORES) % XS, ep % CORES
    z = z_hi * ZL + z_lo
    z_rows, y_rows = ys * CAP, zs * CAP

    def z_peer(t):
        return {"ctx": y * ZL + t % ZL, "ep": (t // ZL) * (XS * CORES) + x * CORES + core}

    def y_peer(t):
        return {"ctx": t * ZL + z_lo, "ep": ep}

    def x_peer(t, c):
        return {"ctx": ctx, "ep": z_hi * (XS * CORES) + (t % XS) * CORES + c}

    after = {"ctx": (ctx + 1) % ctxs, "ep": ep}
    before = {"ctx": (ctx + ctxs - 1) % ctxs, "ep": ep}
    right, left = x_peer(x + 1, core), x_peer(x + XS - 1, core)
    twin = x_peer(x, 1 - core)

    def order(count):
        steps = []
        for i in range(1, count // 2 + 1):
            steps.append(i)
            if count - i != i:
                steps.append(count - i)
        return steps

    barrier = pltpu.get_barrier_semaphore()
    peers = [after, before, right, left, twin]
    peers += [z_peer((z + i) % zs) for i in order(zs)]
    peers += [y_peer((y + i) % ys) for i in order(ys)]
    for peer in peers:
        pl.semaphore_signal(barrier, inc=1, device_id=peer, device_id_type=MESH)

    def local(src, dst, sem):
        pltpu.make_async_copy(src, dst, sem).start()

    def wait(ref, sem):
        pltpu.make_async_copy(ref, ref, sem).wait()

    def send(src, dst, s_sem, r_sem, peer):
        pltpu.make_async_remote_copy(
            src_ref=src, dst_ref=dst, send_sem=s_sem, recv_sem=r_sem,
            device_id=peer, device_id_type=MESH,
        ).start()

    def exchange(src, dst, rows, count, mine, peer, s_sem, r_sem):
        own = pl.ds(pl.multiple_of(mine * rows, rows), rows)
        for i in order(count):
            t = (mine + i) % count
            there = pl.ds(pl.multiple_of(t * rows, rows), rows)
            send(src.at[there], dst.at[own], s_sem, r_sem, peer(t))
        local(src.at[own], dst.at[own], r_sem)

    def sent(src, rows, count, s_sem):
        wait(src.at[pl.ds(0, rows * (count - 1))], s_sem)

    def col(g):
        return pl.ds(pl.multiple_of(g * cols, cols), cols)

    local(go_hbm.at[0], s["go"], s["load_go"])
    own_rows = pl.ds(0, slice_cols)
    for a, (ref, name) in enumerate(((wg_hbm, "wg"), (wu_hbm, "wu"), (wd_hbm, "wd"))):
        local(ref, s[name].at[own_rows], s["load_w"].at[a])

    @pl.loop(0, groups)
    def _(g):
        local(q_hbm.at[0, :, col(g)], s["q"].at[g], s["load_q"])
        local(k_hbm.at[0, :, col(g)], s["kv"].at[0, 0, g], s["load_kv"])
        local(v_hbm.at[0, :, col(g)], s["kv"].at[0, 1, g], s["load_kv"])

    def grid(shape, axis):
        return lax.broadcasted_iota(jnp.int32, shape, axis)

    def across(row):
        return jnp.transpose(jnp.broadcast_to(row.astype(F32), (tokens, tokens)))

    def onehot(mask):
        return jnp.where(mask, 1.0, 0.0).astype(BF16)

    square = (tokens, tokens)
    route_row = route_ref[...].astype(F32)
    same = (jnp.broadcast_to(route_row, square) == across(route_row)) & (
        grid(square, 0) < grid(square, 1)
    )
    rank = jnp.sum(jnp.where(same, 1.0, 0.0), axis=0, keepdims=True).astype(jnp.int32)
    expert = route_ref[...]
    bits_zh, bits_zl = ZH.bit_length() - 1, ZL.bit_length() - 1
    dest_y = lax.shift_right_logical(expert, bits_zh + bits_zl)
    dest_z = (expert & (ZH - 1)) * ZL + (lax.shift_right_logical(expert, bits_zh) & (ZL - 1))
    target = jnp.where(rank < CAP, dest_z * z_rows + dest_y * CAP + rank, -1)
    s["pick"][...] = onehot(jnp.broadcast_to(target, (slots, tokens)) == grid((slots, tokens), 0))
    target_y = jnp.where(rank < CAP, dest_y * y_rows + dest_z * CAP + rank, -1)
    for i, at in enumerate((target, target_y)):
        s["place"][i] = onehot(across(at) == grid((tokens, slots), 1).astype(F32))

    def regroup(index, outer, inner):
        bits_o, bits_i = outer.bit_length() - 1, inner.bit_length() - 1
        o = lax.shift_right_logical(index, bits_i + 1)
        i = lax.shift_right_logical(index, 1) & (inner - 1)
        return i * (outer * CAP) + o * CAP + (index & (CAP - 1))

    pairs = (slots, slots)
    s["perm_f"][...] = onehot(regroup(grid(pairs, 0), ys, zs) == grid(pairs, 1))
    s["perm_r"][...] = onehot(regroup(grid(pairs, 0), zs, ys) == grid(pairs, 1))

    pl.semaphore_wait(barrier, len(peers))

    def send_own(g):
        for part, ref in ((0, k_hbm), (1, v_hbm)):
            send(
                ref.at[0, :, col(g)], s["kv"].at[1, part, g],
                s["kv_s"].at[0, part, g], s["kv_r"].at[0, part, g], after,
            )

    for g in range(min(LEAD, groups)):
        send_own(g)
    send(doc_ref, s["tags"].at[0], s["tag_s"].at[0], s["tag_r"].at[0], after)

    gathered = (s["wg"], s["wu"], s["wd"])

    def part_of(slot):
        return pl.ds(slot * slice_cols, slice_cols)

    def weights_out(a, src):
        ref = gathered[a]
        send(src, ref.at[part_of(2)], s["w_s"].at[a, 0], s["w_r"].at[a, 0], right)
        send(src, ref.at[part_of(4)], s["w_s"].at[a, 1], s["w_r"].at[a, 1], left)
        send(src, ref.at[part_of(1)], s["w_s"].at[a, 2], s["w_r"].at[a, 2], twin)

    first_cols, last_cols = pl.ds(0, width // 2), pl.ds(width // 2, width // 2)

    def weights_relay(a):
        ref = gathered[a]
        wait(ref.at[part_of(2)], s["w_r"].at[a, 0])
        send(
            ref.at[part_of(2), first_cols], ref.at[part_of(6), first_cols],
            s["w_s"].at[a, 3], s["w_r"].at[a, 3], right,
        )
        send(ref.at[part_of(2)], ref.at[part_of(3)], s["w_s"].at[a, 5], s["w_r"].at[a, 5], twin)
        wait(ref.at[part_of(4)], s["w_r"].at[a, 1])
        send(
            ref.at[part_of(4), last_cols], ref.at[part_of(6), last_cols],
            s["w_s"].at[a, 4], s["w_r"].at[a, 4], left,
        )
        send(ref.at[part_of(4)], ref.at[part_of(5)], s["w_s"].at[a, 6], s["w_r"].at[a, 6], twin)

    def weights_last(a):
        ref = gathered[a]
        wait(ref.at[part_of(6), first_cols], s["w_r"].at[a, 3])
        wait(ref.at[part_of(6), last_cols], s["w_r"].at[a, 4])
        send(ref.at[part_of(6)], ref.at[part_of(7)], s["w_s"].at[a, 7], s["w_r"].at[a, 7], twin)

    def weights_in(a):
        ref = gathered[a]
        for slot, r in ((1, 2), (3, 5), (5, 6), (7, 7)):
            wait(ref.at[part_of(slot)], s["w_r"].at[a, r])
        for k in (0, 1, 2, 5, 6, 7):
            wait(ref.at[part_of(0)], s["w_s"].at[a, k])
        wait(ref.at[part_of(0), first_cols], s["w_s"].at[a, 3])
        wait(ref.at[part_of(0), last_cols], s["w_s"].at[a, 4])

    for a, ref in ((2, wd_hbm), (0, wg_hbm), (1, wu_hbm)):
        weights_out(a, ref)

    wait(s["go"], s["load_go"])
    weight_col = across(rw_ref[...])[:, :1]
    for g in range(groups):
        at = pl.ds(g * cols, cols)
        rows = (weight_col * s["go"][:, at].astype(F32)).astype(BF16)
        s["g_send"][g] = nn(s["pick"][...], rows).astype(BF16)

    wait(s["q"], s["load_q"])
    wait(s["kv"].at[0], s["load_kv"])
    scale = 1.0 / math.sqrt(HEAD)

    def attend(g):
        for h in range(GROUP_HEADS):
            at = slice(h * HEAD, (h + 1) * HEAD)
            query = s["q"][g][:, at]
            scores = [
                nt(query, s["kv"][d, 0, g][:, at]) * scale + s["bias"][d] for d in range(3)
            ]
            top = jnp.max(
                jnp.maximum(jnp.maximum(scores[0], scores[1]), scores[2]), axis=-1, keepdims=True
            )
            raised = [jnp.exp(one - top) for one in scores]
            total = jnp.sum(raised[0] + raised[1] + raised[2], axis=-1, keepdims=True)
            share = 1.0 / total
            mixed = None
            for d in range(3):
                term = nn((raised[d] * share).astype(BF16), s["kv"][d, 1, g][:, at])
                mixed = term if mixed is None else mixed + term
            s["hid"][g, :, at] = mixed.astype(BF16)
        s["h_send"][g] = nn(s["pick"][...], s["hid"][g]).astype(BF16)

    @pl.loop(0, groups + 4)
    def _(step):
        @pl.when(step < groups)
        def _():
            for part in range(2):
                here = s["kv"].at[1, part, step]
                wait(here, s["kv_r"].at[0, part, step])
                send(
                    here, s["kv"].at[2, part, step],
                    s["kv_s"].at[1, part, step], s["kv_r"].at[1, part, step], after,
                )

        @pl.when(step + LEAD < groups)
        def _():
            send_own(step + LEAD)

        @pl.when(step == 0)
        def _():
            wait(s["tags"].at[0], s["tag_r"].at[0])
            send(s["tags"].at[0], s["tags"].at[1], s["tag_s"].at[1], s["tag_r"].at[1], after)

        @pl.when(step == 1)
        def _():
            wait(s["tags"].at[1], s["tag_r"].at[1])
            doc_col = across(doc_ref[...])
            for d in range(3):
                row = doc_ref[...] if d == 0 else s["tags"][d - 1]
                seen = row.astype(F32) - jnp.where(ctx >= d, 0.0, 1e6)
                open_ = doc_col == jnp.broadcast_to(seen, square)
                if d == 0:
                    open_ = open_ & (grid(square, 1) <= grid(square, 0))
                s["bias"][d] = jnp.where(open_, 0.0, -1e30)

        @pl.when((step >= 2) & (step < groups + 2))
        def _():
            g = step - 2
            for part in range(2):
                wait(s["kv"].at[2, part, g], s["kv_r"].at[1, part, g])
            attend(g)
            exchange(
                s["h_send"].at[g], s["h_z"].at[g], z_rows, zs, z, z_peer,
                s["hz_s"].at[g], s["hz_r"].at[g],
            )
            exchange(
                s["g_send"].at[g], s["g_z"].at[g], z_rows, zs, z, z_peer,
                s["gz_s"].at[g], s["gz_r"].at[g],
            )

        @pl.when(step >= 4)
        def _():
            g = step - 4
            wait(s["g_z"].at[g], s["gz_r"].at[g])
            s["g_mid"][g] = nn(s["perm_f"][...], s["g_z"][g]).astype(BF16)
            exchange(
                s["g_mid"].at[g], s["g_y"].at[:, col(g)], y_rows, ys, y, y_peer,
                s["gy_s"].at[g], s["gy_r"].at[g],
            )
            wait(s["h_z"].at[g], s["hz_r"].at[g])
            s["h_mid"][g] = nn(s["perm_f"][...], s["h_z"][g]).astype(BF16)
            exchange(
                s["h_mid"].at[g], s["h_y"].at[g], y_rows, ys, y, y_peer,
                s["hy_s"].at[g], s["hy_r"].at[g],
            )

        for a, when in ((2, 2), (0, 4), (1, 6)):

            @pl.when(step == min(when, groups))
            def _():
                weights_relay(a)

        for a, when in ((2, 2), (0, 1)):

            @pl.when(step == groups + 3 - when)
            def _():
                weights_last(a)

    squares = None
    for g in range(groups):
        one = s["hid"][g].astype(F32)
        one = jnp.sum(one * one, axis=-1, keepdims=True)
        squares = one if squares is None else squares + one
    inv_rms = lax.rsqrt(squares * (1.0 / width) + 1e-06)

    weights_last(1)

    def all_here(a):
        wait(gathered[a].at[own_rows], s["load_w"].at[a])
        weights_in(a)

    for g in range(groups):
        wait(s["g_y"].at[:, pl.ds(g * cols, cols)], s["gy_r"].at[g])
    all_here(2)

    def units(part):
        return pl.ds(pl.multiple_of(part * half, half), half)

    @pl.loop(0, HALVES)
    def _(part):
        s["d_act"][part] = nt(s["g_y"][...], s["wd"][units(part), :])

    squares = None
    for g in range(groups):
        wait(s["h_y"].at[g], s["hy_r"].at[g])
        one = s["h_y"][g].astype(F32)
        one = jnp.sum(one * one, axis=-1, keepdims=True)
        squares = one if squares is None else squares + one
    inv_there = lax.rsqrt(squares * (1.0 / width) + 1e-06)
    for g in range(groups):
        at = pl.ds(g * cols, cols)
        s["normed"][:, at] = (s["h_y"][g].astype(F32) * inv_there * gain_ref[:, at]).astype(BF16)
    all_here(0)
    all_here(1)

    @pl.loop(0, HALVES)
    def _(part):
        gate_pre = nt(s["normed"][...], s["wg"][units(part), :])
        up_pre = nt(s["normed"][...], s["wu"][units(part), :])
        grad_act = s["d_act"][part]
        sg = 1.0 / (1.0 + jnp.exp(-gate_pre))
        s["d_gate"][part] = (
            grad_act * up_pre * (sg * (1.0 + gate_pre * (1.0 - sg)))
        ).astype(BF16)
        s["d_up"][part] = (grad_act * (gate_pre * sg)).astype(BF16)

    ways = (
        (y_rows, ys, y, y_peer, z_rows, zs, z, z_peer, "perm_r"),
        (z_rows, zs, z, z_peer, y_rows, ys, y, y_peer, "perm_f"),
    )

    @pl.loop(0, groups // 2)
    def _(pair):
        for way, (rows, count, mine, peer, *_) in enumerate(ways):
            g = 2 * pair + way
            total = None
            for part in range(HALVES):
                here = pl.ds(part * half, half)
                for rows_in, ref in ((s["d_gate"], s["wg"]), (s["d_up"], s["wu"])):
                    term = nn(rows_in[part], ref[here, col(g)])
                    total = term if total is None else total + term
            total = total.astype(BF16)
            if way:
                total = nn(s["perm_r"][...], total).astype(BF16)
            s["r_send"][g] = total
            exchange(
                s["r_send"].at[g], s["r_one"].at[g], rows, count, mine, peer,
                s["r1_s"].at[g], s["r1_r"].at[g],
            )

    @pl.loop(0, groups // 2)
    def _(pair):
        for way, (*_, rows, count, mine, peer, perm) in enumerate(ways):
            g = 2 * pair + way
            wait(s["r_one"].at[g], s["r1_r"].at[g])
            s["r_mid"][g] = nn(s[perm][...], s["r_one"][g]).astype(BF16)
            exchange(
                s["r_mid"].at[g], s["r_two"].at[g], rows, count, mine, peer,
                s["r2_s"].at[g], s["r2_r"].at[g],
            )

    along = None
    for g in range(groups):
        wait(s["r_two"].at[g], s["r2_r"].at[g])
        gained = nn(s["place"][g % 2], s["r_two"][g]) * gain_ref[:, pl.ds(g * cols, cols)]
        s["gained"][g] = gained
        one = jnp.sum(s["hid"][g].astype(F32) * gained, axis=-1, keepdims=True)
        along = one if along is None else along + one
    slope = inv_rms * inv_rms * inv_rms * (along * (1.0 / width))
    for g in range(groups):
        at = pl.ds(g * cols, cols)
        s["out_v"][g] = (
            s["go"][:, at].astype(F32)
            + inv_rms * s["gained"][g]
            - s["hid"][g].astype(F32) * slope
        ).astype(BF16)
        local(s["out_v"].at[g], out_hbm.at[0, :, at], s["store"])

    @pl.loop(0, groups)
    def _(g):
        for hop in range(2):
            for part in range(2):
                wait(s["kv"].at[hop, part, g], s["kv_s"].at[hop, part, g])
        sent(s["g_send"].at[g], z_rows, zs, s["gz_s"].at[g])
        sent(s["g_mid"].at[g], y_rows, ys, s["gy_s"].at[g])
        sent(s["h_send"].at[g], z_rows, zs, s["hz_s"].at[g])
        sent(s["h_mid"].at[g], y_rows, ys, s["hy_s"].at[g])

    @pl.loop(0, groups // 2)
    def _(pair):
        for way, (rows, count, _, _, rows_2, count_2, *_) in enumerate(ways):
            g = 2 * pair + way
            sent(s["r_send"].at[g], rows, count, s["r1_s"].at[g])
            sent(s["r_mid"].at[g], rows_2, count_2, s["r2_s"].at[g])

    for hop in range(2):
        wait(s["tags"].at[hop], s["tag_s"].at[hop])
    wait(s["out_v"], s["store"])


def shards(
    queries, keys, values, doc_ids, routes, route_weight, norm_gain, w_gate, w_up, w_down, grad_out
):
    tokens, width = queries.shape[1:]
    ys = lax.axis_size("ctx") // ZL
    scratch = scratch_of(tokens, width, w_gate.shape[1], ys)
    small = pl.BlockSpec(memory_space=pltpu.VMEM)
    large = pl.BlockSpec(memory_space=pl.ANY)
    return pl.pallas_call(
        functools.partial(kernel, tuple(scratch)),
        out_shape=jax.ShapeDtypeStruct(grad_out.shape, BF16),
        in_specs=[small] * 4 + [large] * 7,
        out_specs=large,
        scratch_shapes=list(scratch.values()),
        compiler_params=pltpu.CompilerParams(
            collective_id=0, has_side_effects=True, vmem_limit_bytes=60 * 1024 * 1024
        ),
        name="layer",
    )(
        doc_ids,
        routes.reshape(1, tokens),
        route_weight.reshape(1, tokens),
        norm_gain.reshape(1, width),
        queries, keys, values, grad_out, w_gate.T, w_up.T, w_down,
    )


def solution(mesh):
    rows = P("ep", "ctx", None)
    in_specs = (
        rows, rows, rows, P("ep", "ctx"), rows, rows, P(),
        P(None, ("ctx", "ep")), P(None, ("ctx", "ep")), P(("ctx", "ep"), None), rows,
    )
    return jax.shard_map(shards, mesh=mesh, in_specs=in_specs, out_specs=rows, check_vma=False)
```

```python
import functools
import math

import jax
import jax.numpy as jnp
from jax import lax
from jax.experimental import pallas as pl
from jax.experimental.pallas import tpu as pltpu
from jax.sharding import PartitionSpec as P

HEADS = 16
HEAD = 128
CAP = 2
ZL = 4
ZH = 2
XS = 4
CORES = 2
SLICES = XS * CORES
GROUP_HEADS = 2
LEAD = 3
HALVES = 2

F32 = jnp.float32
BF16 = jnp.bfloat16
MESH = pl.DeviceIdType.MESH


def nn(a, b):
    return lax.dot_general(a, b, (((1,), (0,)), ((), ())), preferred_element_type=F32)


def nt(a, b):
    return lax.dot_general(a, b, (((1,), (1,)), ((), ())), preferred_element_type=F32)


def scratch_of(tokens, width, slice_cols, ys):
    zs = ZL * ZH
    slots = ys * zs * CAP
    cols = GROUP_HEADS * HEAD
    groups = width // cols
    hidden_units = SLICES * slice_cols
    half = hidden_units // HALVES
    dma = pltpu.SemaphoreType.DMA
    chunked = pltpu.VMEM((groups, slots, cols), BF16)
    flat = pltpu.VMEM((slots, width), BF16)
    weights = pltpu.VMEM((hidden_units, width), BF16)
    return dict(
        q=pltpu.VMEM((groups, tokens, cols), BF16),
        kv=pltpu.VMEM((3, 2, groups, tokens, cols), BF16),
        tags=pltpu.VMEM((2, 1, tokens), jnp.int32),
        go=pltpu.VMEM((tokens, width), BF16),
        bias=pltpu.VMEM((3, tokens, tokens), F32),
        pick=pltpu.VMEM((slots, tokens), BF16),
        place=pltpu.VMEM((2, tokens, slots), BF16),
        perm_f=pltpu.VMEM((slots, slots), BF16),
        perm_r=pltpu.VMEM((slots, slots), BF16),
        g_send=chunked, g_z=chunked, g_mid=chunked, g_y=flat,
        hid=pltpu.VMEM((groups, tokens, cols), BF16),
        h_send=chunked, h_z=chunked, h_mid=chunked, h_y=chunked,
        wg=weights, wu=weights, wd=weights,
        normed=flat,
        d_act=pltpu.VMEM((HALVES, slots, half), F32),
        d_gate=pltpu.VMEM((HALVES, slots, half), BF16),
        d_up=pltpu.VMEM((HALVES, slots, half), BF16),
        r_send=chunked, r_one=chunked, r_mid=chunked, r_two=chunked,
        gained=pltpu.VMEM((groups, tokens, cols), F32),
        out_v=pltpu.VMEM((groups, tokens, cols), BF16),
        load_q=dma, load_kv=dma, load_go=dma, load_w=dma((3,)), store=dma,
        kv_s=dma((2, 2, groups)), kv_r=dma((2, 2, groups)),
        tag_s=dma((2,)), tag_r=dma((2,)),
        gz_s=dma((groups,)), gz_r=dma((groups,)), gy_s=dma((groups,)), gy_r=dma((groups,)),
        hz_s=dma((groups,)), hz_r=dma((groups,)), hy_s=dma((groups,)), hy_r=dma((groups,)),
        r1_s=dma((groups,)), r1_r=dma((groups,)), r2_s=dma((groups,)), r2_r=dma((groups,)),
        w_s=dma((3, 8)), w_r=dma((3, 8)),
    )


def kernel(
    names, doc_ref, route_ref, rw_ref, gain_ref,
    q_hbm, k_hbm, v_hbm, go_hbm, wg_hbm, wu_hbm, wd_hbm, out_hbm, *scratch,
):
    s = dict(zip(names, scratch))
    groups, tokens, cols = s["q"].shape
    slots = s["pick"].shape[0]
    width = groups * cols
    slice_cols = wd_hbm.shape[0]
    half = s["d_gate"].shape[2]
    ctx, ep = lax.axis_index("ctx"), lax.axis_index("ep")
    ctxs = lax.axis_size("ctx")
    ys, zs = ctxs // ZL, ZL * ZH
    y, z_lo = ctx // ZL, ctx % ZL
    z_hi, x, core = ep // (XS * CORES), (ep // CORES) % XS, ep % CORES
    z = z_hi * ZL + z_lo
    z_rows, y_rows = ys * CAP, zs * CAP

    def z_peer(t):
        return {"ctx": y * ZL + t % ZL, "ep": (t // ZL) * (XS * CORES) + x * CORES + core}

    def y_peer(t):
        return {"ctx": t * ZL + z_lo, "ep": ep}

    def x_peer(t, c):
        return {"ctx": ctx, "ep": z_hi * (XS * CORES) + (t % XS) * CORES + c}

    after = {"ctx": (ctx + 1) % ctxs, "ep": ep}
    before = {"ctx": (ctx + ctxs - 1) % ctxs, "ep": ep}
    right, left = x_peer(x + 1, core), x_peer(x + XS - 1, core)
    twin = x_peer(x, 1 - core)

    def order(count):
        steps = []
        for i in range(1, count // 2 + 1):
            steps.append(i)
            if count - i != i:
                steps.append(count - i)
        return steps[::-1]

    barrier = pltpu.get_barrier_semaphore()
    peers = [after, before, right, left, twin]
    peers += [z_peer((z + i) % zs) for i in order(zs)]
    peers += [y_peer((y + i) % ys) for i in order(ys)]
    for peer in peers:
        pl.semaphore_signal(barrier, inc=1, device_id=peer, device_id_type=MESH)

    def local(src, dst, sem):
        pltpu.make_async_copy(src, dst, sem).start()

    def wait(ref, sem):
        pltpu.make_async_copy(ref, ref, sem).wait()

    def send(src, dst, s_sem, r_sem, peer):
        pltpu.make_async_remote_copy(
            src_ref=src, dst_ref=dst, send_sem=s_sem, recv_sem=r_sem,
            device_id=peer, device_id_type=MESH,
        ).start()

    def exchange(src, dst, rows, count, mine, peer, s_sem, r_sem):
        own = pl.ds(pl.multiple_of(mine * rows, rows), rows)
        for i in order(count):
            t = (mine + i) % count
            there = pl.ds(pl.multiple_of(t * rows, rows), rows)
            send(src.at[there], dst.at[own], s_sem, r_sem, peer(t))
        local(src.at[own], dst.at[own], r_sem)

    def sent(src, rows, count, s_sem):
        wait(src.at[pl.ds(0, rows * (count - 1))], s_sem)

    def col(g):
        return pl.ds(pl.multiple_of(g * cols, cols), cols)

    local(go_hbm.at[0], s["go"], s["load_go"])
    own_rows = pl.ds(0, slice_cols)
    for a, (ref, name) in enumerate(((wg_hbm, "wg"), (wu_hbm, "wu"), (wd_hbm, "wd"))):
        local(ref, s[name].at[own_rows], s["load_w"].at[a])

    @pl.loop(0, groups)
    def _(g):
        local(q_hbm.at[0, :, col(g)], s["q"].at[g], s["load_q"])
        local(k_hbm.at[0, :, col(g)], s["kv"].at[0, 0, g], s["load_kv"])
        local(v_hbm.at[0, :, col(g)], s["kv"].at[0, 1, g], s["load_kv"])

    def grid(shape, axis):
        return lax.broadcasted_iota(jnp.int32, shape, axis)

    def across(row):
        return jnp.transpose(jnp.broadcast_to(row.astype(F32), (tokens, tokens)))

    def onehot(mask):
        return jnp.where(mask, 1.0, 0.0).astype(BF16)

    square = (tokens, tokens)
    route_row = route_ref[...].astype(F32)
    same = (jnp.broadcast_to(route_row, square) == across(route_row)) & (
        grid(square, 0) < grid(square, 1)
    )
    rank = jnp.sum(jnp.where(same, 1.0, 0.0), axis=0, keepdims=True).astype(jnp.int32)
    expert = route_ref[...]
    bits_zh, bits_zl = ZH.bit_length() - 1, ZL.bit_length() - 1
    dest_y = lax.shift_right_logical(expert, bits_zh + bits_zl)
    dest_z = (expert & (ZH - 1)) * ZL + (lax.shift_right_logical(expert, bits_zh) & (ZL - 1))
    target = jnp.where(rank < CAP, dest_z * z_rows + dest_y * CAP + rank, -1)
    s["pick"][...] = onehot(jnp.broadcast_to(target, (slots, tokens)) == grid((slots, tokens), 0))
    target_y = jnp.where(rank < CAP, dest_y * y_rows + dest_z * CAP + rank, -1)
    for i, at in enumerate((target, target_y)):
        s["place"][i] = onehot(across(at) == grid((tokens, slots), 1).astype(F32))

    def regroup(index, outer, inner):
        bits_o, bits_i = outer.bit_length() - 1, inner.bit_length() - 1
        o = lax.shift_right_logical(index, bits_i + 1)
        i = lax.shift_right_logical(index, 1) & (inner - 1)
        return i * (outer * CAP) + o * CAP + (index & (CAP - 1))

    pairs = (slots, slots)
    s["perm_f"][...] = onehot(regroup(grid(pairs, 0), ys, zs) == grid(pairs, 1))
    s["perm_r"][...] = onehot(regroup(grid(pairs, 0), zs, ys) == grid(pairs, 1))

    pl.semaphore_wait(barrier, len(peers))

    def send_own(g):
        for part, ref in ((0, k_hbm), (1, v_hbm)):
            send(
                ref.at[0, :, col(g)], s["kv"].at[1, part, g],
                s["kv_s"].at[0, part, g], s["kv_r"].at[0, part, g], after,
            )

    for g in range(min(LEAD, groups)):
        send_own(g)
    send(doc_ref, s["tags"].at[0], s["tag_s"].at[0], s["tag_r"].at[0], after)

    gathered = (s["wg"], s["wu"], s["wd"])

    def part_of(slot):
        return pl.ds(slot * slice_cols, slice_cols)

    def weights_out(a, src):
        ref = gathered[a]
        send(src, ref.at[part_of(2)], s["w_s"].at[a, 0], s["w_r"].at[a, 0], right)
        send(src, ref.at[part_of(4)], s["w_s"].at[a, 1], s["w_r"].at[a, 1], left)
        send(src, ref.at[part_of(1)], s["w_s"].at[a, 2], s["w_r"].at[a, 2], twin)

    first_cols, last_cols = pl.ds(0, width // 2), pl.ds(width // 2, width // 2)

    def weights_relay(a):
        ref = gathered[a]
        wait(ref.at[part_of(2)], s["w_r"].at[a, 0])
        send(
            ref.at[part_of(2), first_cols], ref.at[part_of(6), first_cols],
            s["w_s"].at[a, 3], s["w_r"].at[a, 3], right,
        )
        send(ref.at[part_of(2)], ref.at[part_of(3)], s["w_s"].at[a, 5], s["w_r"].at[a, 5], twin)
        wait(ref.at[part_of(4)], s["w_r"].at[a, 1])
        send(
            ref.at[part_of(4), last_cols], ref.at[part_of(6), last_cols],
            s["w_s"].at[a, 4], s["w_r"].at[a, 4], left,
        )
        send(ref.at[part_of(4)], ref.at[part_of(5)], s["w_s"].at[a, 6], s["w_r"].at[a, 6], twin)

    def weights_last(a):
        ref = gathered[a]
        wait(ref.at[part_of(6), first_cols], s["w_r"].at[a, 3])
        wait(ref.at[part_of(6), last_cols], s["w_r"].at[a, 4])
        send(ref.at[part_of(6)], ref.at[part_of(7)], s["w_s"].at[a, 7], s["w_r"].at[a, 7], twin)

    def weights_in(a):
        ref = gathered[a]
        for slot, r in ((1, 2), (3, 5), (5, 6), (7, 7)):
            wait(ref.at[part_of(slot)], s["w_r"].at[a, r])
        for k in (0, 1, 2, 5, 6, 7):
            wait(ref.at[part_of(0)], s["w_s"].at[a, k])
        wait(ref.at[part_of(0), first_cols], s["w_s"].at[a, 3])
        wait(ref.at[part_of(0), last_cols], s["w_s"].at[a, 4])

    for a, ref in ((2, wd_hbm), (0, wg_hbm), (1, wu_hbm)):
        weights_out(a, ref)

    wait(s["go"], s["load_go"])
    weight_col = across(rw_ref[...])[:, :1]
    for g in range(groups):
        at = pl.ds(g * cols, cols)
        rows = (weight_col * s["go"][:, at].astype(F32)).astype(BF16)
        s["g_send"][g] = nn(s["pick"][...], rows).astype(BF16)

    wait(s["q"], s["load_q"])
    wait(s["kv"].at[0], s["load_kv"])
    scale = 1.0 / math.sqrt(HEAD)

    def attend(g):
        for h in range(GROUP_HEADS):
            at = slice(h * HEAD, (h + 1) * HEAD)
            query = s["q"][g][:, at]
            scores = [
                nt(query, s["kv"][d, 0, g][:, at]) * scale + s["bias"][d] for d in range(3)
            ]
            top = jnp.max(
                jnp.maximum(jnp.maximum(scores[0], scores[1]), scores[2]), axis=-1, keepdims=True
            )
            raised = [jnp.exp(one - top) for one in scores]
            total = jnp.sum(raised[0] + raised[1] + raised[2], axis=-1, keepdims=True)
            share = 1.0 / total
            mixed = None
            for d in range(3):
                term = nn((raised[d] * share).astype(BF16), s["kv"][d, 1, g][:, at])
                mixed = term if mixed is None else mixed + term
            s["hid"][g, :, at] = mixed.astype(BF16)
        s["h_send"][g] = nn(s["pick"][...], s["hid"][g]).astype(BF16)

    def send_g(g):
        exchange(
            s["g_send"].at[g], s["g_z"].at[g], z_rows, zs, z, z_peer,
            s["gz_s"].at[g], s["gz_r"].at[g],
        )

    @pl.loop(0, groups + 4)
    def _(step):
        @pl.when(step < groups)
        def _():
            for part in range(2):
                here = s["kv"].at[1, part, step]
                wait(here, s["kv_r"].at[0, part, step])
                send(
                    here, s["kv"].at[2, part, step],
                    s["kv_s"].at[1, part, step], s["kv_r"].at[1, part, step], after,
                )

        @pl.when(step + LEAD < groups)
        def _():
            send_own(step + LEAD)

        @pl.when(step == 0)
        def _():
            wait(s["tags"].at[0], s["tag_r"].at[0])
            send(s["tags"].at[0], s["tags"].at[1], s["tag_s"].at[1], s["tag_r"].at[1], after)

        @pl.when(step == 1)
        def _():
            wait(s["tags"].at[1], s["tag_r"].at[1])
            doc_col = across(doc_ref[...])
            for d in range(3):
                row = doc_ref[...] if d == 0 else s["tags"][d - 1]
                seen = row.astype(F32) - jnp.where(ctx >= d, 0.0, 1e6)
                open_ = doc_col == jnp.broadcast_to(seen, square)
                if d == 0:
                    open_ = open_ & (grid(square, 1) <= grid(square, 0))
                s["bias"][d] = jnp.where(open_, 0.0, -1e30)

        @pl.when((step >= 2) & (step < groups + 2))
        def _():
            g = step - 2
            send_g(g)
            for part in range(2):
                wait(s["kv"].at[2, part, g], s["kv_r"].at[1, part, g])
            attend(g)
            exchange(
                s["h_send"].at[g], s["h_z"].at[g], z_rows, zs, z, z_peer,
                s["hz_s"].at[g], s["hz_r"].at[g],
            )

        @pl.when(step >= 4)
        def _():
            g = step - 4
            wait(s["g_z"].at[g], s["gz_r"].at[g])
            s["g_mid"][g] = nn(s["perm_f"][...], s["g_z"][g]).astype(BF16)
            exchange(
                s["g_mid"].at[g], s["g_y"].at[:, col(g)], y_rows, ys, y, y_peer,
                s["gy_s"].at[g], s["gy_r"].at[g],
            )
            wait(s["h_z"].at[g], s["hz_r"].at[g])
            s["h_mid"][g] = nn(s["perm_f"][...], s["h_z"][g]).astype(BF16)
            exchange(
                s["h_mid"].at[g], s["h_y"].at[g], y_rows, ys, y, y_peer,
                s["hy_s"].at[g], s["hy_r"].at[g],
            )

        for a, when in ((2, 2), (0, 4), (1, 6)):

            @pl.when(step == min(when, groups))
            def _():
                weights_relay(a)

        for a, when in ((2, 2), (0, 1)):

            @pl.when(step == groups + 3 - when)
            def _():
                weights_last(a)

    squares = None
    for g in range(groups):
        one = s["hid"][g].astype(F32)
        one = jnp.sum(one * one, axis=-1, keepdims=True)
        squares = one if squares is None else squares + one
    inv_rms = lax.rsqrt(squares * (1.0 / width) + 1e-06)

    weights_last(1)

    def all_here(a):
        wait(gathered[a].at[own_rows], s["load_w"].at[a])
        weights_in(a)

    for g in range(groups):
        wait(s["g_y"].at[:, pl.ds(g * cols, cols)], s["gy_r"].at[g])
    all_here(2)

    def units(part):
        return pl.ds(pl.multiple_of(part * half, half), half)

    @pl.loop(0, HALVES)
    def _(part):
        s["d_act"][part] = nt(s["g_y"][...], s["wd"][units(part), :])

    squares = None
    for g in range(groups):
        wait(s["h_y"].at[g], s["hy_r"].at[g])
        one = s["h_y"][g].astype(F32)
        one = jnp.sum(one * one, axis=-1, keepdims=True)
        squares = one if squares is None else squares + one
    inv_there = lax.rsqrt(squares * (1.0 / width) + 1e-06)
    for g in range(groups):
        at = pl.ds(g * cols, cols)
        s["normed"][:, at] = (s["h_y"][g].astype(F32) * inv_there * gain_ref[:, at]).astype(BF16)
    all_here(0)
    all_here(1)

    @pl.loop(0, HALVES)
    def _(part):
        gate_pre = nt(s["normed"][...], s["wg"][units(part), :])
        up_pre = nt(s["normed"][...], s["wu"][units(part), :])
        grad_act = s["d_act"][part]
        sg = 1.0 / (1.0 + jnp.exp(-gate_pre))
        s["d_gate"][part] = (
            grad_act * up_pre * (sg * (1.0 + gate_pre * (1.0 - sg)))
        ).astype(BF16)
        s["d_up"][part] = (grad_act * (gate_pre * sg)).astype(BF16)

    ways = (
        (y_rows, ys, y, y_peer, z_rows, zs, z, z_peer, "perm_r"),
        (z_rows, zs, z, z_peer, y_rows, ys, y, y_peer, "perm_f"),
    )

    @pl.loop(0, groups // 2)
    def _(pair):
        for way, (rows, count, mine, peer, *_) in enumerate(ways):
            g = 2 * pair + way
            total = None
            for part in range(HALVES):
                here = pl.ds(part * half, half)
                for rows_in, ref in ((s["d_gate"], s["wg"]), (s["d_up"], s["wu"])):
                    term = nn(rows_in[part], ref[here, col(g)])
                    total = term if total is None else total + term
            total = total.astype(BF16)
            if way:
                total = nn(s["perm_r"][...], total).astype(BF16)
            s["r_send"][g] = total
            exchange(
                s["r_send"].at[g], s["r_one"].at[g], rows, count, mine, peer,
                s["r1_s"].at[g], s["r1_r"].at[g],
            )

    @pl.loop(0, groups // 2)
    def _(pair):
        for way, (*_, rows, count, mine, peer, perm) in enumerate(ways):
            g = 2 * pair + way
            wait(s["r_one"].at[g], s["r1_r"].at[g])
            s["r_mid"][g] = nn(s[perm][...], s["r_one"][g]).astype(BF16)
            exchange(
                s["r_mid"].at[g], s["r_two"].at[g], rows, count, mine, peer,
                s["r2_s"].at[g], s["r2_r"].at[g],
            )

    along = None
    for g in range(groups):
        wait(s["r_two"].at[g], s["r2_r"].at[g])
        gained = nn(s["place"][g % 2], s["r_two"][g]) * gain_ref[:, pl.ds(g * cols, cols)]
        s["gained"][g] = gained
        one = jnp.sum(s["hid"][g].astype(F32) * gained, axis=-1, keepdims=True)
        along = one if along is None else along + one
    slope = inv_rms * inv_rms * inv_rms * (along * (1.0 / width))
    for g in range(groups):
        at = pl.ds(g * cols, cols)
        s["out_v"][g] = (
            s["go"][:, at].astype(F32)
            + inv_rms * s["gained"][g]
            - s["hid"][g].astype(F32) * slope
        ).astype(BF16)
        local(s["out_v"].at[g], out_hbm.at[0, :, at], s["store"])

    @pl.loop(0, groups)
    def _(g):
        for hop in range(2):
            for part in range(2):
                wait(s["kv"].at[hop, part, g], s["kv_s"].at[hop, part, g])
        sent(s["g_send"].at[g], z_rows, zs, s["gz_s"].at[g])
        sent(s["g_mid"].at[g], y_rows, ys, s["gy_s"].at[g])
        sent(s["h_send"].at[g], z_rows, zs, s["hz_s"].at[g])
        sent(s["h_mid"].at[g], y_rows, ys, s["hy_s"].at[g])

    @pl.loop(0, groups // 2)
    def _(pair):
        for way, (rows, count, _, _, rows_2, count_2, *_) in enumerate(ways):
            g = 2 * pair + way
            sent(s["r_send"].at[g], rows, count, s["r1_s"].at[g])
            sent(s["r_mid"].at[g], rows_2, count_2, s["r2_s"].at[g])

    for hop in range(2):
        wait(s["tags"].at[hop], s["tag_s"].at[hop])
    wait(s["out_v"], s["store"])


def shards(
    queries, keys, values, doc_ids, routes, route_weight, norm_gain, w_gate, w_up, w_down, grad_out
):
    tokens, width = queries.shape[1:]
    ys = lax.axis_size("ctx") // ZL
    scratch = scratch_of(tokens, width, w_gate.shape[1], ys)
    small = pl.BlockSpec(memory_space=pltpu.VMEM)
    large = pl.BlockSpec(memory_space=pl.ANY)
    return pl.pallas_call(
        functools.partial(kernel, tuple(scratch)),
        out_shape=jax.ShapeDtypeStruct(grad_out.shape, BF16),
        in_specs=[small] * 4 + [large] * 7,
        out_specs=large,
        scratch_shapes=list(scratch.values()),
        compiler_params=pltpu.CompilerParams(
            collective_id=0, has_side_effects=True, vmem_limit_bytes=60 * 1024 * 1024
        ),
        name="layer",
    )(
        doc_ids,
        routes.reshape(1, tokens),
        route_weight.reshape(1, tokens),
        norm_gain.reshape(1, width),
        queries, keys, values, grad_out, w_gate.T, w_up.T, w_down,
    )


def solution(mesh):
    rows = P("ep", "ctx", None)
    in_specs = (
        rows, rows, rows, P("ep", "ctx"), rows, rows, P(),
        P(None, ("ctx", "ep")), P(None, ("ctx", "ep")), P(("ctx", "ep"), None), rows,
    )
    return jax.shard_map(shards, mesh=mesh, in_specs=in_specs, out_specs=rows, check_vma=False)
```

```python
import functools
import math

import jax
import jax.numpy as jnp
from jax import lax
from jax.experimental import pallas as pl
from jax.experimental.pallas import tpu as pltpu
from jax.sharding import PartitionSpec as P

HEADS = 16
HEAD = 128
CAP = 2
ZL = 4
ZH = 2
XS = 4
CORES = 2
SLICES = XS * CORES
GROUP_HEADS = 2
LEAD = 3
G_LAG = 4
G_START = 2
HALVES = 2

F32 = jnp.float32
BF16 = jnp.bfloat16
MESH = pl.DeviceIdType.MESH


def nn(a, b):
    return lax.dot_general(a, b, (((1,), (0,)), ((), ())), preferred_element_type=F32)


def nt(a, b):
    return lax.dot_general(a, b, (((1,), (1,)), ((), ())), preferred_element_type=F32)


def scratch_of(tokens, width, slice_cols, ys):
    zs = ZL * ZH
    slots = ys * zs * CAP
    cols = GROUP_HEADS * HEAD
    groups = width // cols
    hidden_units = SLICES * slice_cols
    half = hidden_units // HALVES
    dma = pltpu.SemaphoreType.DMA
    chunked = pltpu.VMEM((groups, slots, cols), BF16)
    flat = pltpu.VMEM((slots, width), BF16)
    weights = pltpu.VMEM((hidden_units, width), BF16)
    return dict(
        q=pltpu.VMEM((groups, tokens, cols), BF16),
        kv=pltpu.VMEM((3, 2, groups, tokens, cols), BF16),
        tags=pltpu.VMEM((2, 1, tokens), jnp.int32),
        go=pltpu.VMEM((tokens, width), BF16),
        bias=pltpu.VMEM((3, tokens, tokens), F32),
        pick=pltpu.VMEM((2, slots, tokens), BF16),
        place=pltpu.VMEM((2, tokens, slots), BF16),
        perm_f=pltpu.VMEM((slots, slots), BF16),
        perm_r=pltpu.VMEM((slots, slots), BF16),
        g_send=chunked, g_one=chunked, g_mid=chunked, g_two=chunked, g_in=flat,
        hid=pltpu.VMEM((groups, tokens, cols), BF16),
        h_send=chunked, h_z=chunked, h_mid=chunked, h_y=chunked,
        wg=weights, wu=weights, wd=weights,
        normed=flat,
        d_act=pltpu.VMEM((HALVES, slots, half), F32),
        d_gate=pltpu.VMEM((HALVES, slots, half), BF16),
        d_up=pltpu.VMEM((HALVES, slots, half), BF16),
        r_send=chunked, r_one=chunked, r_mid=chunked, r_two=chunked,
        gained=pltpu.VMEM((groups, tokens, cols), F32),
        out_v=pltpu.VMEM((groups, tokens, cols), BF16),
        load_q=dma, load_kv=dma, load_go=dma, load_w=dma((3,)), store=dma,
        kv_s=dma((2, 2, groups)), kv_r=dma((2, 2, groups)),
        tag_s=dma((2,)), tag_r=dma((2,)),
        gz_s=dma((groups,)), gz_r=dma((groups,)), gy_s=dma((groups,)), gy_r=dma((groups,)),
        hz_s=dma((groups,)), hz_r=dma((groups,)), hy_s=dma((groups,)), hy_r=dma((groups,)),
        r1_s=dma((groups,)), r1_r=dma((groups,)), r2_s=dma((groups,)), r2_r=dma((groups,)),
        w_s=dma((3, 8)), w_r=dma((3, 8)),
    )


def kernel(
    names, doc_ref, route_ref, rw_ref, gain_ref,
    q_hbm, k_hbm, v_hbm, go_hbm, wg_hbm, wu_hbm, wd_hbm, out_hbm, *scratch,
):
    s = dict(zip(names, scratch))
    groups, tokens, cols = s["q"].shape
    slots = s["pick"].shape[1]
    width = groups * cols
    slice_cols = wd_hbm.shape[0]
    half = s["d_gate"].shape[2]
    ctx, ep = lax.axis_index("ctx"), lax.axis_index("ep")
    ctxs = lax.axis_size("ctx")
    ys, zs = ctxs // ZL, ZL * ZH
    y, z_lo = ctx // ZL, ctx % ZL
    z_hi, x, core = ep // (XS * CORES), (ep // CORES) % XS, ep % CORES
    z = z_hi * ZL + z_lo
    z_rows, y_rows = ys * CAP, zs * CAP

    def z_peer(t):
        return {"ctx": y * ZL + t % ZL, "ep": (t // ZL) * (XS * CORES) + x * CORES + core}

    def y_peer(t):
        return {"ctx": t * ZL + z_lo, "ep": ep}

    def x_peer(t, c):
        return {"ctx": ctx, "ep": z_hi * (XS * CORES) + (t % XS) * CORES + c}

    after = {"ctx": (ctx + 1) % ctxs, "ep": ep}
    before = {"ctx": (ctx + ctxs - 1) % ctxs, "ep": ep}
    right, left = x_peer(x + 1, core), x_peer(x + XS - 1, core)
    twin = x_peer(x, 1 - core)

    def order(count):
        steps = []
        for i in range(1, count // 2 + 1):
            steps.append(i)
            if count - i != i:
                steps.append(count - i)
        return steps[::-1]

    barrier = pltpu.get_barrier_semaphore()
    peers = [after, before, right, left, twin]
    peers += [z_peer((z + i) % zs) for i in order(zs)]
    peers += [y_peer((y + i) % ys) for i in order(ys)]
    for peer in peers:
        pl.semaphore_signal(barrier, inc=1, device_id=peer, device_id_type=MESH)

    def local(src, dst, sem):
        pltpu.make_async_copy(src, dst, sem).start()

    def wait(ref, sem):
        pltpu.make_async_copy(ref, ref, sem).wait()

    def send(src, dst, s_sem, r_sem, peer):
        pltpu.make_async_remote_copy(
            src_ref=src, dst_ref=dst, send_sem=s_sem, recv_sem=r_sem,
            device_id=peer, device_id_type=MESH,
        ).start()

    def exchange(src, dst, rows, count, mine, peer, s_sem, r_sem):
        own = pl.ds(pl.multiple_of(mine * rows, rows), rows)
        for i in order(count):
            t = (mine + i) % count
            there = pl.ds(pl.multiple_of(t * rows, rows), rows)
            send(src.at[there], dst.at[own], s_sem, r_sem, peer(t))
        local(src.at[own], dst.at[own], r_sem)

    def sent(src, rows, count, s_sem):
        wait(src.at[pl.ds(0, rows * (count - 1))], s_sem)

    def col(g):
        return pl.ds(pl.multiple_of(g * cols, cols), cols)

    local(go_hbm.at[0], s["go"], s["load_go"])
    own_rows = pl.ds(0, slice_cols)
    for a, (ref, name) in enumerate(((wg_hbm, "wg"), (wu_hbm, "wu"), (wd_hbm, "wd"))):
        local(ref, s[name].at[own_rows], s["load_w"].at[a])

    @pl.loop(0, groups)
    def _(g):
        local(q_hbm.at[0, :, col(g)], s["q"].at[g], s["load_q"])
        local(k_hbm.at[0, :, col(g)], s["kv"].at[0, 0, g], s["load_kv"])
        local(v_hbm.at[0, :, col(g)], s["kv"].at[0, 1, g], s["load_kv"])

    def grid(shape, axis):
        return lax.broadcasted_iota(jnp.int32, shape, axis)

    def across(row):
        return jnp.transpose(jnp.broadcast_to(row.astype(F32), (tokens, tokens)))

    def onehot(mask):
        return jnp.where(mask, 1.0, 0.0).astype(BF16)

    square = (tokens, tokens)
    route_row = route_ref[...].astype(F32)
    same = (jnp.broadcast_to(route_row, square) == across(route_row)) & (
        grid(square, 0) < grid(square, 1)
    )
    rank = jnp.sum(jnp.where(same, 1.0, 0.0), axis=0, keepdims=True).astype(jnp.int32)
    expert = route_ref[...]
    bits_zh, bits_zl = ZH.bit_length() - 1, ZL.bit_length() - 1
    dest_y = lax.shift_right_logical(expert, bits_zh + bits_zl)
    dest_z = (expert & (ZH - 1)) * ZL + (lax.shift_right_logical(expert, bits_zh) & (ZL - 1))
    target = jnp.where(rank < CAP, dest_z * z_rows + dest_y * CAP + rank, -1)
    target_y = jnp.where(rank < CAP, dest_y * y_rows + dest_z * CAP + rank, -1)
    for i, at in enumerate((target, target_y)):
        s["pick"][i] = onehot(jnp.broadcast_to(at, (slots, tokens)) == grid((slots, tokens), 0))
        s["place"][i] = onehot(across(at) == grid((tokens, slots), 1).astype(F32))

    def regroup(index, outer, inner):
        bits_o, bits_i = outer.bit_length() - 1, inner.bit_length() - 1
        o = lax.shift_right_logical(index, bits_i + 1)
        i = lax.shift_right_logical(index, 1) & (inner - 1)
        return i * (outer * CAP) + o * CAP + (index & (CAP - 1))

    pairs = (slots, slots)
    s["perm_f"][...] = onehot(regroup(grid(pairs, 0), ys, zs) == grid(pairs, 1))
    s["perm_r"][...] = onehot(regroup(grid(pairs, 0), zs, ys) == grid(pairs, 1))

    pl.semaphore_wait(barrier, len(peers))

    def send_own(g):
        for part, ref in ((0, k_hbm), (1, v_hbm)):
            send(
                ref.at[0, :, col(g)], s["kv"].at[1, part, g],
                s["kv_s"].at[0, part, g], s["kv_r"].at[0, part, g], after,
            )

    for g in range(min(LEAD, groups)):
        send_own(g)
    send(doc_ref, s["tags"].at[0], s["tag_s"].at[0], s["tag_r"].at[0], after)

    gathered = (s["wg"], s["wu"], s["wd"])

    def part_of(slot):
        return pl.ds(slot * slice_cols, slice_cols)

    def weights_out(a, src):
        ref = gathered[a]
        send(src, ref.at[part_of(2)], s["w_s"].at[a, 0], s["w_r"].at[a, 0], right)
        send(src, ref.at[part_of(4)], s["w_s"].at[a, 1], s["w_r"].at[a, 1], left)
        send(src, ref.at[part_of(1)], s["w_s"].at[a, 2], s["w_r"].at[a, 2], twin)

    first_cols, last_cols = pl.ds(0, width // 2), pl.ds(width // 2, width // 2)

    def weights_relay(a):
        ref = gathered[a]
        wait(ref.at[part_of(2)], s["w_r"].at[a, 0])
        send(
            ref.at[part_of(2), first_cols], ref.at[part_of(6), first_cols],
            s["w_s"].at[a, 3], s["w_r"].at[a, 3], right,
        )
        send(ref.at[part_of(2)], ref.at[part_of(3)], s["w_s"].at[a, 5], s["w_r"].at[a, 5], twin)
        wait(ref.at[part_of(4)], s["w_r"].at[a, 1])
        send(
            ref.at[part_of(4), last_cols], ref.at[part_of(6), last_cols],
            s["w_s"].at[a, 4], s["w_r"].at[a, 4], left,
        )
        send(ref.at[part_of(4)], ref.at[part_of(5)], s["w_s"].at[a, 6], s["w_r"].at[a, 6], twin)

    def weights_last(a):
        ref = gathered[a]
        wait(ref.at[part_of(6), first_cols], s["w_r"].at[a, 3])
        wait(ref.at[part_of(6), last_cols], s["w_r"].at[a, 4])
        send(ref.at[part_of(6)], ref.at[part_of(7)], s["w_s"].at[a, 7], s["w_r"].at[a, 7], twin)

    def weights_in(a):
        ref = gathered[a]
        for slot, r in ((1, 2), (3, 5), (5, 6), (7, 7)):
            wait(ref.at[part_of(slot)], s["w_r"].at[a, r])
        for k in (0, 1, 2, 5, 6, 7):
            wait(ref.at[part_of(0)], s["w_s"].at[a, k])
        wait(ref.at[part_of(0), first_cols], s["w_s"].at[a, 3])
        wait(ref.at[part_of(0), last_cols], s["w_s"].at[a, 4])

    for a, ref in ((2, wd_hbm), (0, wg_hbm), (1, wu_hbm)):
        weights_out(a, ref)

    wait(s["go"], s["load_go"])
    weight_col = across(rw_ref[...])[:, :1]
    for g in range(groups):
        at = pl.ds(g * cols, cols)
        rows = (weight_col * s["go"][:, at].astype(F32)).astype(BF16)
        s["g_send"][g] = nn(s["pick"][1], rows).astype(BF16)

    wait(s["q"], s["load_q"])
    wait(s["kv"].at[0], s["load_kv"])
    scale = 1.0 / math.sqrt(HEAD)

    def attend(g):
        for h in range(GROUP_HEADS):
            at = slice(h * HEAD, (h + 1) * HEAD)
            query = s["q"][g][:, at]
            scores = [
                nt(query, s["kv"][d, 0, g][:, at]) * scale + s["bias"][d] for d in range(3)
            ]
            top = jnp.max(
                jnp.maximum(jnp.maximum(scores[0], scores[1]), scores[2]), axis=-1, keepdims=True
            )
            raised = [jnp.exp(one - top) for one in scores]
            total = jnp.sum(raised[0] + raised[1] + raised[2], axis=-1, keepdims=True)
            share = 1.0 / total
            mixed = None
            for d in range(3):
                term = nn((raised[d] * share).astype(BF16), s["kv"][d, 1, g][:, at])
                mixed = term if mixed is None else mixed + term
            s["hid"][g, :, at] = mixed.astype(BF16)
        s["h_send"][g] = nn(s["pick"][0], s["hid"][g]).astype(BF16)

    @pl.loop(0, groups + 4)
    def _(step):
        @pl.when(step < groups)
        def _():
            for part in range(2):
                here = s["kv"].at[1, part, step]
                wait(here, s["kv_r"].at[0, part, step])
                send(
                    here, s["kv"].at[2, part, step],
                    s["kv_s"].at[1, part, step], s["kv_r"].at[1, part, step], after,
                )

        @pl.when(step + LEAD < groups)
        def _():
            send_own(step + LEAD)

        @pl.when(step == 0)
        def _():
            wait(s["tags"].at[0], s["tag_r"].at[0])
            send(s["tags"].at[0], s["tags"].at[1], s["tag_s"].at[1], s["tag_r"].at[1], after)

        @pl.when(step == 1)
        def _():
            wait(s["tags"].at[1], s["tag_r"].at[1])
            doc_col = across(doc_ref[...])
            for d in range(3):
                row = doc_ref[...] if d == 0 else s["tags"][d - 1]
                seen = row.astype(F32) - jnp.where(ctx >= d, 0.0, 1e6)
                open_ = doc_col == jnp.broadcast_to(seen, square)
                if d == 0:
                    open_ = open_ & (grid(square, 1) <= grid(square, 0))
                s["bias"][d] = jnp.where(open_, 0.0, -1e30)

        @pl.when((step >= 2) & (step < groups + 2))
        def _():
            g = step - 2
            for part in range(2):
                wait(s["kv"].at[2, part, g], s["kv_r"].at[1, part, g])
            attend(g)
            exchange(
                s["h_send"].at[g], s["h_z"].at[g], z_rows, zs, z, z_peer,
                s["hz_s"].at[g], s["hz_r"].at[g],
            )

        @pl.when((step >= G_START) & (step < groups + G_START))
        def _():
            g = step - G_START
            exchange(
                s["g_send"].at[g], s["g_one"].at[g], y_rows, ys, y, y_peer,
                s["gy_s"].at[g], s["gy_r"].at[g],
            )

        @pl.when((step >= G_LAG) & (step < groups + G_LAG))
        def _():
            g = step - G_LAG
            wait(s["g_one"].at[g], s["gy_r"].at[g])
            s["g_mid"][g] = nn(s["perm_r"][...], s["g_one"][g]).astype(BF16)
            exchange(
                s["g_mid"].at[g], s["g_two"].at[g], z_rows, zs, z, z_peer,
                s["gz_s"].at[g], s["gz_r"].at[g],
            )

        @pl.when(step >= 4)
        def _():
            g = step - 4
            wait(s["h_z"].at[g], s["hz_r"].at[g])
            s["h_mid"][g] = nn(s["perm_f"][...], s["h_z"][g]).astype(BF16)
            exchange(
                s["h_mid"].at[g], s["h_y"].at[g], y_rows, ys, y, y_peer,
                s["hy_s"].at[g], s["hy_r"].at[g],
            )

        for a, when in ((2, 2), (0, 4), (1, 6)):

            @pl.when(step == min(when, groups))
            def _():
                weights_relay(a)

        for a, when in ((2, 2), (0, 1)):

            @pl.when(step == groups + 3 - when)
            def _():
                weights_last(a)

    squares = None
    for g in range(groups):
        one = s["hid"][g].astype(F32)
        one = jnp.sum(one * one, axis=-1, keepdims=True)
        squares = one if squares is None else squares + one
    inv_rms = lax.rsqrt(squares * (1.0 / width) + 1e-06)

    weights_last(1)

    def all_here(a):
        wait(gathered[a].at[own_rows], s["load_w"].at[a])
        weights_in(a)

    for g in range(groups):
        wait(s["g_two"].at[g], s["gz_r"].at[g])
        at = pl.ds(g * cols, cols)
        s["g_in"][:, at] = nn(s["perm_f"][...], s["g_two"][g]).astype(BF16)
    all_here(2)

    def units(part):
        return pl.ds(pl.multiple_of(part * half, half), half)

    @pl.loop(0, HALVES)
    def _(part):
        s["d_act"][part] = nt(s["g_in"][...], s["wd"][units(part), :])

    squares = None
    for g in range(groups):
        wait(s["h_y"].at[g], s["hy_r"].at[g])
        one = s["h_y"][g].astype(F32)
        one = jnp.sum(one * one, axis=-1, keepdims=True)
        squares = one if squares is None else squares + one
    inv_there = lax.rsqrt(squares * (1.0 / width) + 1e-06)
    for g in range(groups):
        at = pl.ds(g * cols, cols)
        s["normed"][:, at] = (s["h_y"][g].astype(F32) * inv_there * gain_ref[:, at]).astype(BF16)
    all_here(0)
    all_here(1)

    @pl.loop(0, HALVES)
    def _(part):
        gate_pre = nt(s["normed"][...], s["wg"][units(part), :])
        up_pre = nt(s["normed"][...], s["wu"][units(part), :])
        grad_act = s["d_act"][part]
        sg = 1.0 / (1.0 + jnp.exp(-gate_pre))
        s["d_gate"][part] = (
            grad_act * up_pre * (sg * (1.0 + gate_pre * (1.0 - sg)))
        ).astype(BF16)
        s["d_up"][part] = (grad_act * (gate_pre * sg)).astype(BF16)

    ways = (
        (y_rows, ys, y, y_peer, z_rows, zs, z, z_peer, "perm_r"),
        (z_rows, zs, z, z_peer, y_rows, ys, y, y_peer, "perm_f"),
    )

    @pl.loop(0, groups // 2)
    def _(pair):
        for way, (rows, count, mine, peer, *_) in enumerate(ways):
            g = 2 * pair + way
            total = None
            for part in range(HALVES):
                here = pl.ds(part * half, half)
                for rows_in, ref in ((s["d_gate"], s["wg"]), (s["d_up"], s["wu"])):
                    term = nn(rows_in[part], ref[here, col(g)])
                    total = term if total is None else total + term
            total = total.astype(BF16)
            if way:
                total = nn(s["perm_r"][...], total).astype(BF16)
            s["r_send"][g] = total
            exchange(
                s["r_send"].at[g], s["r_one"].at[g], rows, count, mine, peer,
                s["r1_s"].at[g], s["r1_r"].at[g],
            )

    @pl.loop(0, groups // 2)
    def _(pair):
        for way, (*_, rows, count, mine, peer, perm) in enumerate(ways):
            g = 2 * pair + way
            wait(s["r_one"].at[g], s["r1_r"].at[g])
            s["r_mid"][g] = nn(s[perm][...], s["r_one"][g]).astype(BF16)
            exchange(
                s["r_mid"].at[g], s["r_two"].at[g], rows, count, mine, peer,
                s["r2_s"].at[g], s["r2_r"].at[g],
            )

    along = None
    for g in range(groups):
        wait(s["r_two"].at[g], s["r2_r"].at[g])
        gained = nn(s["place"][g % 2], s["r_two"][g]) * gain_ref[:, pl.ds(g * cols, cols)]
        s["gained"][g] = gained
        one = jnp.sum(s["hid"][g].astype(F32) * gained, axis=-1, keepdims=True)
        along = one if along is None else along + one
    slope = inv_rms * inv_rms * inv_rms * (along * (1.0 / width))
    for g in range(groups):
        at = pl.ds(g * cols, cols)
        s["out_v"][g] = (
            s["go"][:, at].astype(F32)
            + inv_rms * s["gained"][g]
            - s["hid"][g].astype(F32) * slope
        ).astype(BF16)
        local(s["out_v"].at[g], out_hbm.at[0, :, at], s["store"])

    @pl.loop(0, groups)
    def _(g):
        for hop in range(2):
            for part in range(2):
                wait(s["kv"].at[hop, part, g], s["kv_s"].at[hop, part, g])
        sent(s["g_send"].at[g], y_rows, ys, s["gy_s"].at[g])
        sent(s["g_mid"].at[g], z_rows, zs, s["gz_s"].at[g])
        sent(s["h_send"].at[g], z_rows, zs, s["hz_s"].at[g])
        sent(s["h_mid"].at[g], y_rows, ys, s["hy_s"].at[g])

    @pl.loop(0, groups // 2)
    def _(pair):
        for way, (rows, count, _, _, rows_2, count_2, *_) in enumerate(ways):
            g = 2 * pair + way
            sent(s["r_send"].at[g], rows, count, s["r1_s"].at[g])
            sent(s["r_mid"].at[g], rows_2, count_2, s["r2_s"].at[g])

    for hop in range(2):
        wait(s["tags"].at[hop], s["tag_s"].at[hop])
    wait(s["out_v"], s["store"])


def shards(
    queries, keys, values, doc_ids, routes, route_weight, norm_gain, w_gate, w_up, w_down, grad_out
):
    tokens, width = queries.shape[1:]
    ys = lax.axis_size("ctx") // ZL
    scratch = scratch_of(tokens, width, w_gate.shape[1], ys)
    small = pl.BlockSpec(memory_space=pltpu.VMEM)
    large = pl.BlockSpec(memory_space=pl.ANY)
    return pl.pallas_call(
        functools.partial(kernel, tuple(scratch)),
        out_shape=jax.ShapeDtypeStruct(grad_out.shape, BF16),
        in_specs=[small] * 4 + [large] * 7,
        out_specs=large,
        scratch_shapes=list(scratch.values()),
        compiler_params=pltpu.CompilerParams(
            collective_id=0, has_side_effects=True, vmem_limit_bytes=60 * 1024 * 1024
        ),
        name="layer",
    )(
        doc_ids,
        routes.reshape(1, tokens),
        route_weight.reshape(1, tokens),
        norm_gain.reshape(1, width),
        queries, keys, values, grad_out, w_gate.T, w_up.T, w_down,
    )


def solution(mesh):
    rows = P("ep", "ctx", None)
    in_specs = (
        rows, rows, rows, P("ep", "ctx"), rows, rows, P(),
        P(None, ("ctx", "ep")), P(None, ("ctx", "ep")), P(("ctx", "ep"), None), rows,
    )
    return jax.shard_map(shards, mesh=mesh, in_specs=in_specs, out_specs=rows, check_vma=False)
```
